512 devices in a mesh: freq: 4 (over x), span: 16 (over z, core), wall: 8 (over y).
Axes of the slice: x: 4, y: 8, z: 8, core: 2. Of those that a mesh axis runs over, the one named last changes fastest.
Arguments:
- amplitudes: float32 [2, 5, 512, 32768], P(None, None, 'wall', ('freq', 'span')), may hold values from -20 to 20
- upstream: float32 [2, 5, 512, 32768], P(None, None, 'wall', ('freq', 'span')), may hold values from -6 to 6
- harmonic_mask: int32 [32768], P(('freq', 'span')), may hold values 0 or 1
- quadratic_coefficients: float32 [5, 5, 5], replicated, may hold values from -1.25 to 1.25
- slab_inverse: float32 [8, 320, 320], P('wall'), may hold values from -1 to 2
- lower_coupling: float32 [8, 5, 5], P('wall'), may hold values from -2.5 to 2.5
- upper_coupling: float32 [8, 5, 5], P('wall'), may hold values from -2.5 to 2.5
- reduced_lower: float32 [8, 10, 10], P('wall'), may hold values from -1 to 1
- reduced_upper: float32 [8, 10, 10], P('wall'), may hold values from -1 to 1
- reduced_pivot: float32 [8, 10, 10], P('wall'), may hold values from -2 to 3
Outputs:
- new_amplitudes: float32 [2, 5, 512, 32768], P(None, None, 'wall', ('freq', 'span'))
- wavenumber_shift: float32 [2, 32768], P(None, ('freq', 'span'))
The draws below stay inside these ranges and needn't reach their ends.
Inputs may be any that keep to these rules, and one draw needn't show every extreme that they name: `harmonic_mask`: 1 marks a retained mode.
All inputs are finite; a program needn't handle non-finite values. No bound on the sum of `harmonic_mask` on one device may be relied on, other than what follows from the above.
Results may differ from the reference program's by a relative error of at most 0.0001.
Values sent between devices are 32-bit elements; how exact they have to be, the bound alone decides.
A program may use at most 64 MiB of HBM per device.

```python
import math
import jax
import jax.numpy as jnp
from jax import lax

V = 5
NF = 128
NB = 256
CY = 64
NY = 512
NM = 32768
N_WALL = 8


def draw_amplitudes(key, part):
    key_rough, key_level = jax.random.split(key, 2)
    levels = jnp.exp(jax.random.uniform(key_level, (1, 1, 1, NF * NB), jnp.float32, math.log(0.3), math.log(3.0)))
    height = 0.5 + jnp.arange(NY, dtype=jnp.float32) / NY
    profile = height[None, None, :, None]
    values = jax.random.normal(key_rough, (2, V, NY, NF * NB), jnp.float32)
    return jnp.clip(values * levels * profile, -20.0, 20.0)


def draw_slab_inverse(key, part):
    extent = V * CY
    noise = jax.random.normal(key, (N_WALL, extent, extent), jnp.float32)
    return jnp.clip(jnp.eye(extent, dtype=jnp.float32)[None] + 0.7 * noise / math.sqrt(extent), -1.0, 2.0)


def draw_reduced_pivot(key, part):
    extent = 2 * V
    noise = jax.random.normal(key, (N_WALL, extent, extent), jnp.float32)
    return jnp.clip(jnp.eye(extent, dtype=jnp.float32)[None] + 0.35 * noise / math.sqrt(extent), -2.0, 3.0)


def touch_ends(values, rng, least, high):
    index_at = [jax.random.randint(jax.random.fold_in(rng, axis), (), 0, length) for axis, length in enumerate(values.shape)]
    widest = values.shape.index(max(values.shape))
    beside = index_at[:widest] + [(index_at[widest] + 1) % values.shape[widest]] + index_at[widest + 1:]
    return values.at[tuple(index_at)].set(least).at[tuple(beside)].set(high)


def level_of(rng, dims, shards, least, largest):
    factor_of = 1.0
    for dim, parts in shards:
        draws = jax.random.uniform(jax.random.fold_in(jax.random.fold_in(rng, 6), dim), (parts,), jnp.float32, least / len(shards), largest / len(shards))
        factor_of = factor_of * jnp.repeat(jnp.exp(draws), dims[dim] // parts).reshape((-1,) + (1,) * (len(dims) - 1 - dim))
    return factor_of


def bell_draw(own_key, dims, width, reach, cuts=(), kind=jnp.bfloat16):
    factor_of = level_of(own_key, dims, cuts, -0.22, 0.18) if cuts else 1.0
    result = jax.random.normal(own_key, dims, jnp.float32) * width * factor_of
    return jnp.minimum(jnp.maximum(result, -reach), reach).astype(kind)


def setup_inputs(seed: int = 0) -> dict:
    seeds = jax.random.split(jax.random.key(seed), 11)
    amplitudes = draw_amplitudes(jax.random.fold_in(seeds[10], 71), 0)
    upstream = bell_draw(seeds[1], (2, V, NY, NM), 1.0, 6.0, ((2, 8), (3, 64)), jnp.float32)
    harmonic_mask = touch_ends((jax.random.randint(seeds[2], (NM,), 0, 4) < 3).astype(jnp.int32), jax.random.fold_in(seeds[2], 1), 0, 1)
    quadratic_coefficients = bell_draw(seeds[3], (V, V, V), (V * V) ** -0.5, 1.25, (), jnp.float32)
    slab_inverse = draw_slab_inverse(jax.random.fold_in(seeds[10], 71), 0)
    lower_coupling = bell_draw(seeds[5], (N_WALL, V, V), V ** -0.5, 2.5, ((0, 8),), jnp.float32)
    upper_coupling = bell_draw(seeds[6], (N_WALL, V, V), V ** -0.5, 2.5, ((0, 8),), jnp.float32)
    reduced_lower = bell_draw(seeds[7], (N_WALL, 2 * V, 2 * V), (6 * V) ** -0.5, 1.0, ((0, 8),), jnp.float32)
    reduced_upper = bell_draw(seeds[8], (N_WALL, 2 * V, 2 * V), (6 * V) ** -0.5, 1.0, ((0, 8),), jnp.float32)
    reduced_pivot = draw_reduced_pivot(jax.random.fold_in(seeds[10], 71), 0)
    return dict(amplitudes=amplitudes, upstream=upstream, harmonic_mask=harmonic_mask, quadratic_coefficients=quadratic_coefficients, slab_inverse=slab_inverse, lower_coupling=lower_coupling, upper_coupling=upper_coupling, reduced_lower=reduced_lower, reduced_upper=reduced_upper, reduced_pivot=reduced_pivot)


epsilon = 1e-06

def apply_left(matrix, vectors):
    return jnp.einsum('ij,cjm->cim', matrix, vectors, precision=lax.Precision.HIGHEST)

def quadratic(field, coefficients):
    weights = coefficients * (1.0 - jnp.eye(coefficients.shape[0], dtype=jnp.float32))[None]
    total = jnp.zeros_like(field)
    for source_var in range(field.shape[0]):
        mixed = jnp.einsum('wb,bynt->wynt', weights[:, source_var, :], field, precision=lax.Precision.HIGHEST)
        total = total + field[source_var][None] * mixed
    return total

def reference(amplitudes, upstream, harmonic_mask, quadratic_coefficients, slab_inverse, lower_coupling, upper_coupling, reduced_lower, reduced_upper, reduced_pivot):
    keep = harmonic_mask.astype(jnp.float32)
    kept = amplitudes * keep
    scale = 1.0 / math.sqrt(NF * NB)

    def slab_solve(items):
        block, source, inverse = items
        spectrum = lax.complex(block[0], block[1]).reshape(V, CY, NF, NB)
        field = jnp.real(jnp.fft.ifft2(spectrum, axes=(2, 3))) * (NF * NB * scale)
        forcing = jnp.fft.fft2(quadratic(field, quadratic_coefficients), axes=(2, 3)) * scale
        forcing = forcing.reshape(V, CY, NF * NB)
        right_side = (jnp.stack([jnp.real(forcing), jnp.imag(forcing)]) + source) * keep
        flat = right_side.reshape(2, V * CY, NF * NB)
        solved = jnp.einsum('ij,cjm->cim', inverse, flat, precision=lax.Precision.HIGHEST)
        return solved.reshape(2, V, CY, NF * NB)

    def slabs(array):
        return jnp.moveaxis(array.reshape(2, V, N_WALL, CY, NF * NB), 2, 0)
    solved = lax.map(slab_solve, (slabs(kept), slabs(upstream), slab_inverse))
    bounds = jnp.concatenate([solved[:, :, :, 0], solved[:, :, :, CY - 1]], axis=2)
    zeros = jnp.zeros_like(bounds[0])
    ahead = []
    carried = zeros
    for wall_index in range(N_WALL):
        carried = bounds[wall_index] - apply_left(reduced_lower[wall_index], carried)
        ahead.append(carried)
    interface = [zeros] * N_WALL
    carried = zeros
    for wall_index in range(N_WALL - 1, -1, -1):
        carried = apply_left(reduced_pivot[wall_index], ahead[wall_index] - apply_left(reduced_upper[wall_index], carried))
        interface[wall_index] = carried
    pieces = []
    for wall_index in range(N_WALL):
        below = interface[wall_index - 1][:, V:] if wall_index > 0 else zeros[:, V:]
        above = interface[wall_index + 1][:, :V] if wall_index < N_WALL - 1 else zeros[:, :V]
        columns = slab_inverse[wall_index].reshape(V * CY, V, CY)
        pushed = apply_left(columns[:, :, 0], apply_left(lower_coupling[wall_index], below))
        pushed = pushed + apply_left(columns[:, :, CY - 1], apply_left(upper_coupling[wall_index], above))
        pieces.append(solved[wall_index] - pushed.reshape(2, V, CY, NF * NB))
    new_amplitudes = jnp.concatenate(pieces, axis=2)
    change = new_amplitudes - kept
    real_part = lax.optimization_barrier(jnp.sum(kept[0] * change[0] + kept[1] * change[1], axis=(0, 1)))
    imag_part = lax.optimization_barrier(jnp.sum(kept[0] * change[1] - kept[1] * change[0], axis=(0, 1)))
    weight = lax.optimization_barrier(jnp.sum(kept * kept, axis=(0, 1, 2))) + epsilon
    wavenumber_shift = jnp.stack([imag_part / weight, -real_part / weight])
    return (new_amplitudes, wavenumber_shift)
```

```python
import functools
import math

import jax
import jax.numpy as jnp
import numpy as np
from jax import lax
from jax.experimental import pallas as pl
from jax.experimental.pallas import tpu as pltpu
from jax.sharding import PartitionSpec as P

MESH = pl.DeviceIdType.MESH
V = 5
CY = 64
NF = 128
NB = 256
GROUP = 64
WALL = 8
LANES = 2 * V * CY
MESSAGE = 8 * V
EXT = V * CY
epsilon = 1e-06
HIGHEST = lax.Precision.HIGHEST
NT = (((1,), (1,)), ((), ()))
NN = (((1,), (0,)), ((), ()))


def split(x):
    high = x.astype(jnp.bfloat16)
    low = (x - high.astype(jnp.float32)).astype(jnp.bfloat16)
    return high, low


def product(a, b, dims):
    (ah, al), (bh, bl) = a, b
    dot = functools.partial(
        lax.dot_general, dimension_numbers=dims, preferred_element_type=jnp.float32
    )
    return dot(ah, bh) + (dot(ah, bl) + dot(al, bh))


def exact(a, b, dims=NN):
    return lax.dot_general(
        a, b, dimension_numbers=dims, precision=HIGHEST, preferred_element_type=jnp.float32
    )


def tables():
    scale = 1.0 / math.sqrt(NF * NB)
    n = np.arange(2 * NB)
    z = 4 * (n // 8) + n % 4
    d = (n // 4) % 2
    phase = 2.0 * np.pi * ((z[:, None] * np.arange(NB)[None, :]) % NB) / NB
    cos, sin = np.cos(phase), np.sin(phase)
    odd = (d == 1)[:, None]
    span = np.concatenate([np.where(odd, sin, cos), np.where(odd, cos, -sin)], axis=1)
    j, t = np.arange(GROUP), np.arange(GROUP)
    inverse, forward = [], []
    for r in range(2):
        phase = 2.0 * np.pi * ((t[:, None] * (2 * j + r)[None, :]) % NF) / NF
        pair = np.concatenate([np.cos(phase), -np.sin(phase)], axis=1) * scale
        inverse.append(pair)
        forward.append(pair.T)
    out = []
    for table in (span, np.concatenate(inverse, axis=1), np.concatenate(forward, axis=1)):
        table = table.astype(np.float32)
        high = table.astype(jnp.bfloat16)
        low = (table - high.astype(np.float32)).astype(jnp.bfloat16)
        out += [high, low]
    return out


def kernel(
    amp_ref, up_ref, mask_ref, quad_ref, inv_ref, lower_ref, upper_ref, rlow_ref, rup_ref, rpiv_ref,
    th_ref, tl_ref, ch_ref, cl_ref, dh_ref, dl_ref,
    new_ref, shift_ref,
    kh, kl, send1, recv1, send2, recv2, invs, ph, pl_, su, et, acc, zmat, nmat, mm,
    wsend, wrecv, msend, mrecv, bsend, brecv, lsend, lrecv, nsend, nrecv, invb_h, invb_l,
    s1, r1, s2, r2, sw, rw,
):
    f, s, w = lax.axis_index("freq"), lax.axis_index("span"), lax.axis_index("wall")
    chip, core = s // 2, s % 2
    me = f * 16 + s
    barrier = pltpu.get_barrier_semaphore()

    def peer(i):
        i = jnp.where(i >= 7, i + 1, i)
        n = 7 - i % 8
        dz = (n % 2) * ((n + 1) // 2) + (1 - n % 2) * ((8 - n // 2) % 8)
        df, dc = (i // 8) % 4, i // 32
        return (f + df) % 4, ((chip + dz) % 8) * 2 + (core + dc) % 2

    def greet(i, carry):
        pf, ps = peer(i)
        pl.semaphore_signal(barrier, inc=1, device_id={"freq": pf, "span": ps}, device_id_type=MESH)
        return carry

    lax.fori_loop(0, GROUP - 1, greet, 0)
    for i in range(1, WALL):
        pl.semaphore_signal(barrier, inc=1, device_id={"wall": (w + i) % WALL}, device_id_type=MESH)

    def tile(index):
        return pl.ds(pl.multiple_of(MESSAGE * index, 8), MESSAGE)

    def exchange(src, dst, ssem, rsem):
        def go(i, carry):
            pf, ps = peer(i)
            p = pf * 16 + ps
            pltpu.make_async_remote_copy(
                src_ref=src.at[tile(p)], dst_ref=dst.at[tile(me)], send_sem=ssem.at[p],
                recv_sem=rsem.at[me], device_id={"freq": pf, "span": ps}, device_id_type=MESH,
            ).start()
            return carry

        lax.fori_loop(0, GROUP - 1, go, 0)

    def finish(src, dst, ssem, rsem):
        def done(i, carry):
            pf, ps = peer(i)
            p = pf * 16 + ps
            pltpu.make_async_remote_copy(
                src_ref=src.at[tile(p)], dst_ref=dst.at[tile(p)], send_sem=ssem.at[p],
                recv_sem=rsem.at[p], device_id={"freq": pf, "span": ps}, device_id_type=MESH,
            ).wait()
            return carry

        lax.fori_loop(0, GROUP - 1, done, 0)

    def wall_copy(step, i, src, dst, inbound=False):
        p = (w + i) % WALL
        return pltpu.make_async_remote_copy(
            src_ref=src(p), dst_ref=dst.at[p if inbound else w], send_sem=sw.at[step, p],
            recv_sem=rw.at[step, p if inbound else w], device_id={"wall": p}, device_id_type=MESH,
        )

    keep = mask_ref[...].astype(jnp.float32)

    weight = jnp.zeros((1, 2 * NB), jnp.float32)
    for c in range(2):
        for v in range(V):
            block = amp_ref[c, v] * keep
            weight = weight + jnp.sum(block * block, axis=0, keepdims=True)
            high, low = split(block)
            for r in range(2):
                rows = pl.ds(v * 2 * CY + r * CY, CY)
                cols = pl.ds(c * NB, NB)
                kh[rows, cols] = high[:, r * NB : (r + 1) * NB]
                kl[rows, cols] = low[:, r * NB : (r + 1) * NB]

    def spectral(q, carry):
        rows = pl.ds(pl.multiple_of(128 * q, 128), 128)
        found = product((th_ref[rows, :], tl_ref[rows, :]), (kh[...], kl[...]), NT)
        for p in range(16):
            for v in range(V):
                at = pl.multiple_of(16 * MESSAGE * q + MESSAGE * p + 8 * v, 8)
                send1[pl.ds(at, 8), :] = found[8 * p : 8 * p + 8, 128 * v : 128 * v + 128]
        return carry

    lax.fori_loop(0, 4, spectral, 0)
    pl.semaphore_wait(barrier, GROUP - 1 + WALL - 1)
    exchange(send1, recv1, s1, r1)
    recv1[tile(me), :] = send1[tile(me), :]

    msend[...] = jnp.zeros_like(msend)
    msend[0:10, 0:10] = rlow_ref[0]
    msend[16:26, 0:10] = rup_ref[0]
    msend[32:42, 0:10] = rpiv_ref[0]
    for q in range(4):
        msend[48 + q : 49 + q, :] = weight[:, 128 * q : 128 * (q + 1)]
    for i in range(1, WALL):
        wall_copy(0, i, lambda p: msend, mrecv).start()
    mrecv[w] = msend[...]

    invs[...] = jnp.zeros_like(invs)
    invs[:, 0:EXT] = inv_ref[0]
    row = lax.broadcasted_iota(jnp.int32, (16, 384), 0)
    col = lax.broadcasted_iota(jnp.int32, (16, 384), 1)
    ends = jnp.zeros((16, 384), jnp.float32)
    for v in range(V):
        for q in range(V):
            first = (row == q) & (col == v * CY)
            last = (row == V + q) & (col == v * CY + CY - 1)
            ends = jnp.where(first, lower_ref[0, v, q], ends)
            ends = jnp.where(last, upper_ref[0, v, q], ends)
    et[...] = ends
    zt = exact(et[...], invs[...], NT)
    zmat[...] = exact(invs[...], et[...], NT)
    for c in range(2):
        kept = (amp_ref[c] * keep).reshape(EXT, 2 * NB)
        found = exact(zt, kept)
        for q in range(4):
            wsend[q, c] = found[:, 128 * q : 128 * (q + 1)]
    for i in range(1, WALL):
        wall_copy(1, i, lambda p: wsend.at[p % 4], wrecv).start()
    wrecv[w] = wsend[w % 4]

    lower_half = lax.broadcasted_iota(jnp.int32, (EXT, 128), 1) < CY
    for v in range(V):
        here = invs[:, 128 * (v // 2) : 128 * (v // 2) + 128]
        there = pltpu.roll(here, CY, 1)
        for r in range(2):
            inside = lower_half if r == 0 else jnp.logical_not(lower_half)
            high, low = split(jnp.where(inside, here if v % 2 == r else there, 0.0))
            ph[r, :, 128 * v : 128 * (v + 1)] = high
            pl_[r, :, 128 * v : 128 * (v + 1)] = low
    inv_h, inv_l = split(inv_ref[0])
    for c in range(2):
        source = split(up_ref[c].reshape(EXT, 2 * NB))
        su[:, c * 2 * NB : (c + 1) * 2 * NB] = product((inv_h, inv_l), source, NN)

    for i in range(1, WALL):
        wall_copy(0, i, lambda p: msend, mrecv, True).wait()
    row = lax.broadcasted_iota(jnp.int32, (16, 128), 0)
    col = lax.broadcasted_iota(jnp.int32, (16, 128), 1)
    ahead = []
    for i in range(WALL):
        unit = jnp.where((col == 16 * i + row) & (row < 2 * V), 1.0, 0.0)
        ahead.append(unit if i == 0 else unit - exact(mrecv[i, 0:16, 0:16], ahead[-1]))
    interface = [None] * WALL
    for i in range(WALL - 1, -1, -1):
        value = ahead[i]
        if i < WALL - 1:
            value = value - exact(mrecv[i, 16:32, 0:16], interface[i + 1])
        interface[i] = exact(mrecv[i, 32:48, 0:16], value)
    for i in range(WALL):
        need = jnp.zeros((16, 128), jnp.float32)
        if i > 0:
            need = jnp.where(row < V, pltpu.roll(interface[i - 1], 16 - V, 0), need)
        if i < WALL - 1:
            need = jnp.where((row >= V) & (row < 2 * V), pltpu.roll(interface[i + 1], V, 0), need)
        mm[16 * i : 16 * (i + 1), :] = need
    total_weight = mrecv[0, 48:56, :]
    for i in range(1, WALL):
        total_weight = total_weight + mrecv[i, 48:56, :]
    for i in range(1, WALL):
        wall_copy(1, i, lambda p: wsend.at[p % 4], wrecv, True).wait()

    finish(send1, recv1, s1, r1)
    half = lax.broadcasted_iota(jnp.int32, (GROUP, 128), 1) < CY
    sign = jnp.where(half, 1.0, -1.0)
    wide = lax.broadcasted_iota(jnp.int32, (128, LANES), 1) % 128 < CY
    halves = lax.broadcasted_iota(jnp.int32, (GROUP, LANES), 1) % 128 < CY
    for z in range(4):
        picked = jnp.concatenate([
            jnp.concatenate([
                recv1[pl.ds(8 * v + 4 * d + z, GROUP, stride=MESSAGE), :] for v in range(V)
            ], axis=1) for d in range(2)
        ], axis=0)
        stacked = jnp.concatenate(
            [jnp.where(wide, picked, 0.0), jnp.where(wide, 0.0, picked)], axis=0
        )
        mixed = product((ch_ref[...], cl_ref[...]), split(stacked), NN)
        field = []
        for v in range(V):
            x = mixed[:, 128 * v : 128 * (v + 1)]
            field.append(pltpu.roll(x, CY, 1) + sign * x)
        force = [jnp.zeros((GROUP, 128), jnp.float32) for _ in range(V)]
        for a in range(V):
            for b in range(a + 1, V):
                both = field[a] * field[b]
                for o in range(V):
                    force[o] = force[o] + (quad_ref[o, a, b] + quad_ref[o, b, a]) * both
        folded = jnp.concatenate([pltpu.roll(x, CY, 1) + sign * x for x in force], axis=1)
        stacked = jnp.concatenate(
            [jnp.where(halves, folded, 0.0), jnp.where(halves, 0.0, folded)], axis=0
        )
        back = product((dh_ref[...], dl_ref[...]), split(stacked), NN)
        for v in range(V):
            for d in range(2):
                send2[pl.ds(8 * v + 4 * d + z, GROUP, stride=MESSAGE), :] = back[
                    GROUP * d : GROUP * (d + 1), 128 * v : 128 * (v + 1)
                ]
    exchange(send2, recv2, s2, r2)
    recv2[tile(me), :] = send2[tile(me), :]

    for r in range(2):
        invb_h[r] = jnp.zeros((16, LANES), jnp.bfloat16)
        invb_l[r] = jnp.zeros((16, LANES), jnp.bfloat16)
        for v in range(V):
            for e in range(2):
                at = v * CY + e * (CY - 1)
                invb_h[r, e * V + v : e * V + v + 1, :] = ph[r, at : at + 1, :]
                invb_l[r, e * V + v : e * V + v + 1, :] = pl_[r, at : at + 1, :]
    finish(send2, recv2, s2, r2)

    landed = recv2[...].reshape(GROUP, V, 8, 128)
    arrived = split(
        jnp.concatenate([landed[:, v].reshape(2 * NB, 128) for v in range(V)], axis=1)
    )
    table = (th_ref[...], tl_ref[...])
    for r in range(2):
        edge = product((invb_h[r], invb_l[r]), arrived, NT)
        edge = product(split(edge), table, NN)
        for c in range(2):
            for q in range(2):
                at = r * NB + q * 128
                part = edge[:, c * NB + q * 128 : c * NB + (q + 1) * 128]
                for e in range(2):
                    for v in range(V):
                        o = v * CY + e * (CY - 1)
                        bsend[c * 4 + r * 2 + q, e * V + v : e * V + v + 1, :] = (
                            part[e * V + v : e * V + v + 1, :]
                            + su[o : o + 1, c * 2 * NB + at : c * 2 * NB + at + 128]
                        ) * keep[:, at : at + 128]
    for q in range(WALL):
        bsend[q, 2 * V : 16, :] = jnp.zeros((16 - 2 * V, 128), jnp.float32)
    for i in range(1, WALL):
        wall_copy(2, i, lambda p: bsend.at[p], brecv).start()
    brecv[w] = bsend[w]

    for r in range(2):
        solved = product(split(product((ph[r], pl_[r]), arrived, NT)), table, NN)
        for c in range(2):
            at = c * 2 * NB + r * NB
            acc[:, at : at + NB] = (
                solved[:, c * NB : (c + 1) * NB] + su[:, at : at + NB]
            ) * keep[:, r * NB : (r + 1) * NB]
    real = jnp.zeros((1, 2 * NB), jnp.float32)
    imag = jnp.zeros((1, 2 * NB), jnp.float32)
    for v in range(V):
        rows = slice(v * CY, (v + 1) * CY)
        k0, k1 = amp_ref[0, v] * keep, amp_ref[1, v] * keep
        c0, c1 = acc[rows, 0 : 2 * NB] - k0, acc[rows, 2 * NB : 4 * NB] - k1
        real = real + jnp.sum(k0 * c0 + k1 * c1, axis=0, keepdims=True)
        imag = imag + jnp.sum(k0 * c1 - k1 * c0, axis=0, keepdims=True)
    for q in range(4):
        lsend[q : q + 1, :] = real[:, 128 * q : 128 * (q + 1)]
        lsend[4 + q : 5 + q, :] = imag[:, 128 * q : 128 * (q + 1)]
    for i in range(1, WALL):
        wall_copy(3, i, lambda p: lsend, lrecv).start()
    lrecv[w] = lsend[...]

    for i in range(1, WALL):
        wall_copy(2, i, lambda p: bsend.at[p], brecv, True).wait()
    need = exact(mm[...], brecv[...].reshape(16 * WALL, 128))
    part = w // 4
    same = wrecv[:, part].reshape(16 * WALL, 128)
    other = wrecv[:, 1 - part].reshape(16 * WALL, 128)
    turn = (2 * part - 1).astype(jnp.float32)
    real = jnp.sum(same * need, axis=0, keepdims=True)
    imag = jnp.sum(other * need, axis=0, keepdims=True) * turn
    nsend[...] = need.reshape(WALL, 16, 128)
    for i in range(WALL):
        nsend[i, 10:11, :] = real
        nsend[i, 11:12, :] = imag
    for i in range(1, WALL):
        wall_copy(4, i, lambda p: nsend.at[p], nrecv).start()
    nrecv[w] = nsend[w]
    for i in range(1, WALL):
        wall_copy(3, i, lambda p: lsend, lrecv, True).wait()
    inner = lrecv[0]
    for i in range(1, WALL):
        inner = inner + lrecv[i]
    for i in range(1, WALL):
        wall_copy(4, i, lambda p: nsend.at[p], nrecv, True).wait()

    for q in range(WALL):
        nmat[:, 128 * q : 128 * (q + 1)] = nrecv[q]
    zsplit = split(zmat[...])
    for c in range(2):
        cols = slice(c * 2 * NB, (c + 1) * 2 * NB)
        pushed = product(zsplit, split(nmat[:, cols]), NN)
        new_ref[c] = (acc[:, cols] - pushed).reshape(V, CY, 2 * NB)
    for q in range(4):
        real = inner[q : q + 1, :] - nrecv[q, 10:11, :] - nrecv[4 + q, 10:11, :]
        imag = inner[4 + q : 5 + q, :] - nrecv[q, 11:12, :] - nrecv[4 + q, 11:12, :]
        size = total_weight[q : q + 1, :] + epsilon
        shift_ref[0:1, 128 * q : 128 * (q + 1)] = imag / size
        shift_ref[1:2, 128 * q : 128 * (q + 1)] = -real / size


def solution(mesh):
    consts = tables()

    def local(
        amplitudes, upstream, harmonic_mask, quadratic_coefficients, slab_inverse,
        lower_coupling, upper_coupling, reduced_lower, reduced_upper, reduced_pivot,
    ):
        vmem = pl.BlockSpec(memory_space=pltpu.VMEM)
        smem = pl.BlockSpec(memory_space=pltpu.SMEM)
        f32, bf16 = jnp.float32, jnp.bfloat16
        modes = amplitudes.shape[3]
        return pl.pallas_call(
            kernel,
            out_shape=(
                jax.ShapeDtypeStruct(amplitudes.shape, f32),
                jax.ShapeDtypeStruct((2, modes), f32),
            ),
            in_specs=[vmem, vmem, vmem, smem, vmem, smem, smem, vmem, vmem, vmem] + [vmem] * 6,
            out_specs=(vmem, vmem),
            scratch_shapes=[
                pltpu.VMEM((LANES, 2 * NB), bf16),
                pltpu.VMEM((LANES, 2 * NB), bf16),
                pltpu.VMEM((GROUP * MESSAGE, 128), f32),
                pltpu.VMEM((GROUP * MESSAGE, 128), f32),
                pltpu.VMEM((GROUP * MESSAGE, 128), f32),
                pltpu.VMEM((GROUP * MESSAGE, 128), f32),
                pltpu.VMEM((EXT, 384), f32),
                pltpu.VMEM((2, EXT, LANES), bf16),
                pltpu.VMEM((2, EXT, LANES), bf16),
                pltpu.VMEM((EXT, 4 * NB), f32),
                pltpu.VMEM((16, 384), f32),
                pltpu.VMEM((EXT, 4 * NB), f32),
                pltpu.VMEM((EXT, 16), f32),
                pltpu.VMEM((16, 4 * NB), f32),
                pltpu.VMEM((128, 128), f32),
                pltpu.VMEM((4, 2, 16, 128), f32),
                pltpu.VMEM((WALL, 2, 16, 128), f32),
                pltpu.VMEM((56, 128), f32),
                pltpu.VMEM((WALL, 56, 128), f32),
                pltpu.VMEM((WALL, 16, 128), f32),
                pltpu.VMEM((WALL, 16, 128), f32),
                pltpu.VMEM((8, 128), f32),
                pltpu.VMEM((WALL, 8, 128), f32),
                pltpu.VMEM((WALL, 16, 128), f32),
                pltpu.VMEM((WALL, 16, 128), f32),
                pltpu.VMEM((2, 16, LANES), bf16),
                pltpu.VMEM((2, 16, LANES), bf16),
                pltpu.SemaphoreType.DMA((GROUP,)),
                pltpu.SemaphoreType.DMA((GROUP,)),
                pltpu.SemaphoreType.DMA((GROUP,)),
                pltpu.SemaphoreType.DMA((GROUP,)),
                pltpu.SemaphoreType.DMA((5, WALL)),
                pltpu.SemaphoreType.DMA((5, WALL)),
            ],
            compiler_params=pltpu.CompilerParams(
                collective_id=0, has_side_effects=True, vmem_limit_bytes=60 << 20
            ),
        )(
            amplitudes, upstream, harmonic_mask.reshape(1, modes), quadratic_coefficients,
            slab_inverse, lower_coupling, upper_coupling, reduced_lower, reduced_upper,
            reduced_pivot, *[jnp.asarray(table) for table in consts],
        )

    placed = (
        P(None, None, "wall", ("freq", "span")),
        P(None, None, "wall", ("freq", "span")),
        P(("freq", "span")),
        P(),
        P("wall", None, None),
        P("wall", None, None),
        P("wall", None, None),
        P("wall", None, None),
        P("wall", None, None),
        P("wall", None, None),
    )
    return jax.shard_map(
        local,
        mesh=mesh,
        in_specs=placed,
        out_specs=(P(None, None, "wall", ("freq", "span")), P(None, ("freq", "span"))),
        check_vma=False,
    )
```

```python
import functools
import math

import jax
import jax.numpy as jnp
import numpy as np
from jax import lax
from jax.experimental import pallas as pl
from jax.experimental.pallas import tpu as pltpu
from jax.sharding import PartitionSpec as P

MESH = pl.DeviceIdType.MESH
V = 5
CY = 64
NF = 128
NB = 256
GROUP = 64
WALL = 8
LANES = 2 * V * CY
MESSAGE = 8 * V
EXT = V * CY
epsilon = 1e-06
HIGHEST = lax.Precision.HIGHEST
NT = (((1,), (1,)), ((), ()))
NN = (((1,), (0,)), ((), ()))


def split(x):
    high = x.astype(jnp.bfloat16)
    low = (x - high.astype(jnp.float32)).astype(jnp.bfloat16)
    return high, low


def product(a, b, dims):
    (ah, al), (bh, bl) = a, b
    dot = functools.partial(
        lax.dot_general, dimension_numbers=dims, preferred_element_type=jnp.float32
    )
    return dot(ah, bh) + (dot(ah, bl) + dot(al, bh))


def exact(a, b, dims=NN):
    return lax.dot_general(
        a, b, dimension_numbers=dims, precision=HIGHEST, preferred_element_type=jnp.float32
    )


def tables():
    scale = 1.0 / math.sqrt(NF * NB)
    n = np.arange(2 * NB)
    z = 4 * (n // 8) + n % 4
    d = (n // 4) % 2
    phase = 2.0 * np.pi * ((z[:, None] * np.arange(NB)[None, :]) % NB) / NB
    cos, sin = np.cos(phase), np.sin(phase)
    odd = (d == 1)[:, None]
    span = np.concatenate([np.where(odd, sin, cos), np.where(odd, cos, -sin)], axis=1)
    t, place = np.arange(GROUP), np.arange(GROUP)
    j = (place // 8 % 4) * 16 + (place % 8) * 2 + place // 32
    inverse, forward = [], []
    for r in range(2):
        phase = 2.0 * np.pi * ((t[:, None] * (2 * j + r)[None, :]) % NF) / NF
        pair = np.stack([np.cos(phase), -np.sin(phase)], axis=1) * scale
        inverse.append(pair.reshape(GROUP, 2, 2, 32))
        forward.append(pair.reshape(GROUP, 2 * GROUP).T)
    inverse = np.stack(inverse).transpose(3, 1, 0, 2, 4).reshape(2, GROUP, 2 * GROUP)
    out = []
    for table in (span, inverse, np.concatenate(forward, axis=1)):
        table = table.astype(np.float32)
        high = table.astype(jnp.bfloat16)
        low = (table - high.astype(np.float32)).astype(jnp.bfloat16)
        out += [high, low]
    return out


def kernel(
    amp_hbm, up_hbm, mask_ref, quad_ref, inv_hbm, lower_ref, upper_ref, rlow_ref, rup_ref, rpiv_ref,
    th_hbm, tl_hbm, ch_ref, cl_ref, dh_ref, dl_ref,
    acc_hbm, zmat, nrecv, inner_ref, weight_ref,
    amp_ref, up_ref, inv_ref, th_ref, tl_ref,
    kh, kl, send1, recv1, send2, recv2, invs, ph, pl_, su, et, acc, mixed, eacc, pacc, mm,
    wsend, wrecv, msend, mrecv, bsend, brecv, lsend, lrecv, nsend, invb_h, invb_l,
    s1, r1, s2, r2, sw, rw, loads,
):
    f, s, w = lax.axis_index("freq"), lax.axis_index("span"), lax.axis_index("wall")
    chip, core = s // 2, s % 2
    me = core * 32 + f * 8 + chip
    barrier = pltpu.get_barrier_semaphore()

    fetch = [
        pltpu.make_async_copy(amp_hbm.at[:, v], amp_ref.at[:, v], loads.at[v]) for v in range(V)
    ]
    for src, dst in ((th_hbm, th_ref), (tl_hbm, tl_ref), (inv_hbm, inv_ref), (up_hbm, up_ref)):
        fetch.append(pltpu.make_async_copy(src, dst, loads.at[len(fetch)]))
    for copy in fetch:
        copy.start()

    def peer(i):
        i = jnp.where(i >= 7, i + 1, i)
        n = 7 - i % 8
        dz = (n % 2) * ((n + 1) // 2) + (1 - n % 2) * ((8 - n // 2) % 8)
        df, dc = (i // 8) % 4, i // 32
        pf, pc, pz = (f + df) % 4, (core + dc) % 2, (chip + dz) % 8
        return {"freq": pf, "span": pz * 2 + pc}, pc * 32 + pf * 8 + pz

    def greet(i, carry):
        pl.semaphore_signal(barrier, inc=1, device_id=peer(i)[0], device_id_type=MESH)
        return carry

    lax.fori_loop(0, GROUP - 1, greet, 0)
    for i in range(1, WALL):
        pl.semaphore_signal(barrier, inc=1, device_id={"wall": (w + i) % WALL}, device_id_type=MESH)

    def tile(index):
        return pl.ds(pl.multiple_of(MESSAGE * index, 8), MESSAGE)

    def message(i, src, dst, ssem, rsem, inbound):
        device, p = peer(i)
        at = p if inbound else me
        return pltpu.make_async_remote_copy(
            src_ref=src.at[tile(p)], dst_ref=dst.at[tile(at)], send_sem=ssem.at[p],
            recv_sem=rsem.at[at], device_id=device, device_id_type=MESH,
        )

    def exchange(*args):
        def go(i, carry):
            message(i, *args, False).start()
            return carry

        lax.fori_loop(0, GROUP - 1, go, 0)

    def arrive(first, last, *args):
        def done(i, carry):
            message(i, *args, True).wait_recv()
            return carry

        lax.fori_loop(first, last, done, 0)

    def sent(*args):
        def done(i, carry):
            message(i, *args, True).wait_send()
            return carry

        lax.fori_loop(0, GROUP - 1, done, 0)

    parts = ((core, 0, 31), (1 - core, 31, GROUP - 1))

    def wall_copy(step, i, src, dst, inbound=False):
        p = (w + i) % WALL
        return pltpu.make_async_remote_copy(
            src_ref=src(p), dst_ref=dst.at[p if inbound else w], send_sem=sw.at[step, p],
            recv_sem=rw.at[step, p if inbound else w], device_id={"wall": p}, device_id_type=MESH,
        )

    keep = mask_ref[...].astype(jnp.float32)

    weight = jnp.zeros((1, 2 * NB), jnp.float32)
    for v in range(V):
        fetch[v].wait()
        for c in range(2):
            block = amp_ref[c, v] * keep
            weight = weight + jnp.sum(block * block, axis=0, keepdims=True)
            high, low = split(block)
            for r in range(2):
                rows = pl.ds(v * 2 * CY + r * CY, CY)
                cols = pl.ds(c * NB, NB)
                kh[rows, cols] = high[:, r * NB : (r + 1) * NB]
                kl[rows, cols] = low[:, r * NB : (r + 1) * NB]

    fetch[V].wait()
    fetch[V + 1].wait()

    def spectral(q, carry):
        rows = pl.ds(pl.multiple_of(128 * q, 128), 128)
        found = product((th_ref[rows, :], tl_ref[rows, :]), (kh[...], kl[...]), NT)
        for p in range(16):
            for v in range(V):
                at = pl.multiple_of(16 * MESSAGE * q + MESSAGE * p + 8 * v, 8)
                send1[pl.ds(at, 8), :] = found[8 * p : 8 * p + 8, 128 * v : 128 * v + 128]
        return carry

    lax.fori_loop(0, 4, spectral, 0)
    pl.semaphore_wait(barrier, GROUP - 1 + WALL - 1)
    exchange(send1, recv1, s1, r1)
    recv1[tile(me), :] = send1[tile(me), :]

    msend[...] = jnp.zeros_like(msend)
    msend[0:10, 0:10] = rlow_ref[:, 0]
    msend[16:26, 0:10] = rup_ref[:, 0]
    msend[32:42, 0:10] = rpiv_ref[:, 0]
    for q in range(4):
        msend[48 + q : 49 + q, :] = weight[:, 128 * q : 128 * (q + 1)]
    for i in range(1, WALL):
        wall_copy(0, i, lambda p: msend, mrecv).start()
    mrecv[w] = msend[...]

    fetch[V + 2].wait()
    invs[...] = jnp.zeros_like(invs)
    invs[:, 0:EXT] = inv_ref[0]
    row = lax.broadcasted_iota(jnp.int32, (16, 384), 0)
    col = lax.broadcasted_iota(jnp.int32, (16, 384), 1)
    ends = jnp.zeros((16, 384), jnp.float32)
    for v in range(V):
        for q in range(V):
            first = (row == q) & (col == v * CY)
            last = (row == V + q) & (col == v * CY + CY - 1)
            ends = jnp.where(first, lower_ref[v, 0, q], ends)
            ends = jnp.where(last, upper_ref[v, 0, q], ends)
    et[...] = ends
    zt = exact(et[...], invs[...], NT)
    zmat[...] = exact(invs[...], et[...], NT)
    for c in range(2):
        kept = (amp_ref[c] * keep).reshape(EXT, 2 * NB)
        found = exact(zt, kept)
        for q in range(4):
            wsend[q, c] = found[:, 128 * q : 128 * (q + 1)]
    for i in range(1, WALL):
        wall_copy(1, i, lambda p: wsend.at[p % 4], wrecv).start()
    wrecv[w] = wsend[w % 4]

    lower_half = lax.broadcasted_iota(jnp.int32, (EXT, 128), 1) < CY
    for v in range(V):
        here = invs[:, 128 * (v // 2) : 128 * (v // 2) + 128]
        there = pltpu.roll(here, CY, 1)
        for r in range(2):
            inside = lower_half if r == 0 else jnp.logical_not(lower_half)
            high, low = split(jnp.where(inside, here if v % 2 == r else there, 0.0))
            ph[r * EXT : (r + 1) * EXT, 128 * v : 128 * (v + 1)] = high
            pl_[r * EXT : (r + 1) * EXT, 128 * v : 128 * (v + 1)] = low
    fetch[V + 3].wait()
    inv_h, inv_l = split(inv_ref[0])
    for c in range(2):
        source = split(up_ref[c].reshape(EXT, 2 * NB))
        su[:, c * 2 * NB : (c + 1) * 2 * NB] = product((inv_h, inv_l), source, NN)

    for i in range(1, WALL):
        wall_copy(0, i, lambda p: msend, mrecv, True).wait()
    row = lax.broadcasted_iota(jnp.int32, (16, 128), 0)
    col = lax.broadcasted_iota(jnp.int32, (16, 128), 1)
    ahead = []
    for i in range(WALL):
        unit = jnp.where((col == 16 * i + row) & (row < 2 * V), 1.0, 0.0)
        ahead.append(unit if i == 0 else unit - exact(mrecv[i, 0:16, 0:16], ahead[-1]))
    interface = [None] * WALL
    for i in range(WALL - 1, -1, -1):
        value = ahead[i]
        if i < WALL - 1:
            value = value - exact(mrecv[i, 16:32, 0:16], interface[i + 1])
        interface[i] = exact(mrecv[i, 32:48, 0:16], value)
    for i in range(WALL):
        need = jnp.zeros((16, 128), jnp.float32)
        if i > 0:
            need = jnp.where(row < V, pltpu.roll(interface[i - 1], 16 - V, 0), need)
        if i < WALL - 1:
            need = jnp.where((row >= V) & (row < 2 * V), pltpu.roll(interface[i + 1], V, 0), need)
        mm[16 * i : 16 * (i + 1), :] = need
    total_weight = mrecv[0, 48:56, :]
    for i in range(1, WALL):
        total_weight = total_weight + mrecv[i, 48:56, :]
    weight_ref[...] = total_weight + epsilon
    invb_h[...] = jnp.zeros_like(invb_h)
    invb_l[...] = jnp.zeros_like(invb_l)
    for r in range(2):
        for e in range(2):
            for v in range(V):
                to, at = 16 * r + e * V + v, r * EXT + v * CY + e * (CY - 1)
                invb_h[to : to + 1, :] = ph[at : at + 1, :]
                invb_l[to : to + 1, :] = pl_[at : at + 1, :]
    for i in range(1, WALL):
        wall_copy(1, i, lambda p: wsend.at[p % 4], wrecv, True).wait()

    half = lax.broadcasted_iota(jnp.int32, (GROUP, 128), 1) < CY
    sign = jnp.where(half, 1.0, -1.0)
    halves = lax.broadcasted_iota(jnp.int32, (GROUP, LANES), 1) % 128 < CY
    for stage, (parity, first, last) in enumerate(parts):
        arrive(first, last, send1, recv1, s1, r1)
        for z in range(4):
            picked = jnp.concatenate([
                jnp.concatenate([
                    recv1[pl.ds(32 * MESSAGE * parity + 8 * v + 4 * d + z, 32, stride=MESSAGE), :]
                    for v in range(V)
                ], axis=1) for d in range(2)
            ], axis=0)
            stacked = jnp.concatenate(
                [jnp.where(halves, picked, 0.0), jnp.where(halves, 0.0, picked)], axis=0
            )
            found = product((ch_ref[parity], cl_ref[parity]), split(stacked), NN)
            mixed[z] = found if stage == 0 else mixed[z] + found
    for z in range(4):
        field = []
        for v in range(V):
            x = mixed[z, :, 128 * v : 128 * (v + 1)]
            field.append(pltpu.roll(x, CY, 1) + sign * x)
        force = [jnp.zeros((GROUP, 128), jnp.float32) for _ in range(V)]
        for a in range(V):
            for b in range(a + 1, V):
                both = field[a] * field[b]
                for o in range(V):
                    force[o] = force[o] + (quad_ref[o, a, b] + quad_ref[o, b, a]) * both
        folded = jnp.concatenate([pltpu.roll(x, CY, 1) + sign * x for x in force], axis=1)
        stacked = jnp.concatenate(
            [jnp.where(halves, folded, 0.0), jnp.where(halves, 0.0, folded)], axis=0
        )
        back = product((dh_ref[...], dl_ref[...]), split(stacked), NN)
        for v in range(V):
            for d in range(2):
                send2[pl.ds(8 * v + 4 * d + z, GROUP, stride=MESSAGE), :] = back[
                    GROUP * d : GROUP * (d + 1), 128 * v : 128 * (v + 1)
                ]
    exchange(send2, recv2, s2, r2)
    recv2[tile(me), :] = send2[tile(me), :]

    sent(send1, recv1, s1, r1)
    for stage, (parity, first, last) in enumerate(parts):
        arrive(first, last, send2, recv2, s2, r2)
        rows = pl.ds(pl.multiple_of(32 * MESSAGE * parity, 8), 32 * MESSAGE)
        landed = recv2[rows, :].reshape(32, V, 8, 128)
        arrived = split(
            jnp.concatenate([landed[:, v].reshape(2 * 128, 128) for v in range(V)], axis=1)
        )
        rows = pl.ds(pl.multiple_of(256 * parity, 256), 256)
        table = (th_ref[rows, :], tl_ref[rows, :])
        found = product((invb_h[...], invb_l[...]), arrived, NT)
        found = product(split(found), table, NN)
        if stage == 0:
            eacc[...] = found
            found = product((ph[...], pl_[...]), arrived, NT)
            pacc[...] = product(split(found), table, NN)
    edges = eacc[...] + found
    for r in range(2):
        edge = edges[16 * r : 16 * (r + 1)]
        for c in range(2):
            for q in range(2):
                at = r * NB + q * 128
                part = edge[:, c * NB + q * 128 : c * NB + (q + 1) * 128]
                for e in range(2):
                    for v in range(V):
                        o = v * CY + e * (CY - 1)
                        bsend[c * 4 + r * 2 + q, e * V + v : e * V + v + 1, :] = (
                            part[e * V + v : e * V + v + 1, :]
                            + su[o : o + 1, c * 2 * NB + at : c * 2 * NB + at + 128]
                        ) * keep[:, at : at + 128]
    for q in range(WALL):
        bsend[q, 2 * V : 16, :] = jnp.zeros((16 - 2 * V, 128), jnp.float32)
    for i in range(1, WALL):
        wall_copy(2, i, lambda p: bsend.at[p], brecv).start()
    brecv[w] = bsend[w]

    pacc[...] += product(split(product((ph[...], pl_[...]), arrived, NT)), table, NN)
    for r in range(2):
        for c in range(2):
            at = c * 2 * NB + r * NB
            acc[:, at : at + NB] = (
                pacc[r * EXT : (r + 1) * EXT, c * NB : (c + 1) * NB] + su[:, at : at + NB]
            ) * keep[:, r * NB : (r + 1) * NB]
    store = pltpu.make_async_copy(acc, acc_hbm, loads.at[V + 4])
    store.start()
    real = jnp.zeros((1, 2 * NB), jnp.float32)
    imag = jnp.zeros((1, 2 * NB), jnp.float32)
    for v in range(V):
        rows = slice(v * CY, (v + 1) * CY)
        k0, k1 = amp_ref[0, v] * keep, amp_ref[1, v] * keep
        c0, c1 = acc[rows, 0 : 2 * NB] - k0, acc[rows, 2 * NB : 4 * NB] - k1
        real = real + jnp.sum(k0 * c0 + k1 * c1, axis=0, keepdims=True)
        imag = imag + jnp.sum(k0 * c1 - k1 * c0, axis=0, keepdims=True)
    for q in range(4):
        lsend[q : q + 1, :] = real[:, 128 * q : 128 * (q + 1)]
        lsend[4 + q : 5 + q, :] = imag[:, 128 * q : 128 * (q + 1)]
    for i in range(1, WALL):
        wall_copy(3, i, lambda p: lsend, lrecv).start()
    lrecv[w] = lsend[...]

    for i in range(1, WALL):
        wall_copy(2, i, lambda p: bsend.at[p], brecv, True).wait()
    need = exact(mm[...], brecv[...].reshape(16 * WALL, 128))
    part = w // 4
    same = wrecv[:, part].reshape(16 * WALL, 128)
    other = wrecv[:, 1 - part].reshape(16 * WALL, 128)
    turn = (2 * part - 1).astype(jnp.float32)
    real = jnp.sum(same * need, axis=0, keepdims=True)
    imag = jnp.sum(other * need, axis=0, keepdims=True) * turn
    nsend[...] = need.reshape(WALL, 16, 128)
    for i in range(WALL):
        nsend[i, 10:11, :] = real
        nsend[i, 11:12, :] = imag
    for i in range(1, WALL):
        wall_copy(4, i, lambda p: nsend.at[p], nrecv).start()
    nrecv[w] = nsend[w]
    for i in range(1, WALL):
        wall_copy(3, i, lambda p: lsend, lrecv, True).wait()
    inner = lrecv[0]
    for i in range(1, WALL):
        inner = inner + lrecv[i]
    inner_ref[...] = inner
    sent(send2, recv2, s2, r2)
    store.wait()
    for i in range(1, WALL):
        wall_copy(4, i, lambda p: nsend.at[p], nrecv, True).wait()


def update(acc_ref, zmat_ref, near_ref, inner_ref, weight_ref, new_ref, shift_ref):
    near = split(jnp.concatenate([near_ref[q] for q in range(WALL)], axis=1))
    value = acc_ref[...] - product(split(zmat_ref[...]), near, NN)
    new_ref[0, 0] = value[:, 0 : 2 * NB]
    new_ref[1, 0] = value[:, 2 * NB : 4 * NB]

    @pl.when(pl.program_id(0) == 0)
    def _():
        for q in range(4):
            real = inner_ref[q : q + 1, :] - near_ref[q, 10:11, :] - near_ref[4 + q, 10:11, :]
            imag = inner_ref[4 + q : 5 + q, :] - near_ref[q, 11:12, :] - near_ref[4 + q, 11:12, :]
            size = weight_ref[q : q + 1, :]
            shift_ref[0:1, 128 * q : 128 * (q + 1)] = imag / size
            shift_ref[1:2, 128 * q : 128 * (q + 1)] = -real / size


def solution(mesh):
    consts = tables()

    def local(
        amplitudes, upstream, harmonic_mask, quadratic_coefficients, slab_inverse,
        lower_coupling, upper_coupling, reduced_lower, reduced_upper, reduced_pivot,
    ):
        vmem = pl.BlockSpec(memory_space=pltpu.VMEM)
        smem = pl.BlockSpec(memory_space=pltpu.SMEM)
        f32, bf16 = jnp.float32, jnp.bfloat16
        modes = amplitudes.shape[3]
        hbm = pl.BlockSpec(memory_space=pl.ANY)

        def turned(block):
            return jnp.transpose(block, (1, 0, 2))

        acc, zmat, near, inner, weight = pl.pallas_call(
            kernel,
            out_shape=(
                jax.ShapeDtypeStruct((EXT, 4 * NB), f32),
                jax.ShapeDtypeStruct((EXT, 16), f32),
                jax.ShapeDtypeStruct((WALL, 16, 128), f32),
                jax.ShapeDtypeStruct((8, 128), f32),
                jax.ShapeDtypeStruct((8, 128), f32),
            ),
            in_specs=[hbm, hbm, vmem, smem, hbm, smem, smem, vmem, vmem, vmem]
            + [hbm, hbm] + [vmem] * 4,
            out_specs=(hbm, vmem, vmem, vmem, vmem),
            scratch_shapes=[
                pltpu.VMEM((2, V, CY, 2 * NB), f32),
                pltpu.VMEM((2, V, CY, 2 * NB), f32),
                pltpu.VMEM((1, EXT, EXT), f32),
                pltpu.VMEM((2 * NB, 2 * NB), bf16),
                pltpu.VMEM((2 * NB, 2 * NB), bf16),
                pltpu.VMEM((LANES, 2 * NB), bf16),
                pltpu.VMEM((LANES, 2 * NB), bf16),
                pltpu.VMEM((GROUP * MESSAGE, 128), f32),
                pltpu.VMEM((GROUP * MESSAGE, 128), f32),
                pltpu.VMEM((GROUP * MESSAGE, 128), f32),
                pltpu.VMEM((GROUP * MESSAGE, 128), f32),
                pltpu.VMEM((EXT, 384), f32),
                pltpu.VMEM((2 * EXT, LANES), bf16),
                pltpu.VMEM((2 * EXT, LANES), bf16),
                pltpu.VMEM((EXT, 4 * NB), f32),
                pltpu.VMEM((16, 384), f32),
                pltpu.VMEM((EXT, 4 * NB), f32),
                pltpu.VMEM((4, GROUP, LANES), f32),
                pltpu.VMEM((32, 2 * NB), f32),
                pltpu.VMEM((2 * EXT, 2 * NB), f32),
                pltpu.VMEM((128, 128), f32),
                pltpu.VMEM((4, 2, 16, 128), f32),
                pltpu.VMEM((WALL, 2, 16, 128), f32),
                pltpu.VMEM((56, 128), f32),
                pltpu.VMEM((WALL, 56, 128), f32),
                pltpu.VMEM((WALL, 16, 128), f32),
                pltpu.VMEM((WALL, 16, 128), f32),
                pltpu.VMEM((8, 128), f32),
                pltpu.VMEM((WALL, 8, 128), f32),
                pltpu.VMEM((WALL, 16, 128), f32),
                pltpu.VMEM((32, LANES), bf16),
                pltpu.VMEM((32, LANES), bf16),
                pltpu.SemaphoreType.DMA((GROUP,)),
                pltpu.SemaphoreType.DMA((GROUP,)),
                pltpu.SemaphoreType.DMA((GROUP,)),
                pltpu.SemaphoreType.DMA((GROUP,)),
                pltpu.SemaphoreType.DMA((5, WALL)),
                pltpu.SemaphoreType.DMA((5, WALL)),
                pltpu.SemaphoreType.DMA((V + 5,)),
            ],
            compiler_params=pltpu.CompilerParams(
                collective_id=0, has_side_effects=True, vmem_limit_bytes=60 << 20
            ),
        )(
            amplitudes, upstream, harmonic_mask.reshape(1, modes), quadratic_coefficients,
            slab_inverse, turned(lower_coupling), turned(upper_coupling), turned(reduced_lower),
            turned(reduced_upper), turned(reduced_pivot),
            *[jnp.asarray(table) for table in consts],
        )
        whole = lambda shape: pl.BlockSpec(shape, lambda v: (0,) * len(shape))
        return pl.pallas_call(
            update,
            grid=(V,),
            out_shape=(
                jax.ShapeDtypeStruct(amplitudes.shape, f32),
                jax.ShapeDtypeStruct((2, modes), f32),
            ),
            in_specs=[
                pl.BlockSpec((CY, 4 * NB), lambda v: (v, 0)),
                pl.BlockSpec((CY, 16), lambda v: (v, 0)),
                whole((WALL, 16, 128)),
                whole((8, 128)),
                whole((8, 128)),
            ],
            out_specs=(
                pl.BlockSpec((2, 1, CY, 2 * NB), lambda v: (0, v, 0, 0)),
                whole((2, modes)),
            ),
        )(acc, zmat, near, inner, weight)

    placed = (
        P(None, None, "wall", ("freq", "span")),
        P(None, None, "wall", ("freq", "span")),
        P(("freq", "span")),
        P(),
        P("wall", None, None),
        P("wall", None, None),
        P("wall", None, None),
        P("wall", None, None),
        P("wall", None, None),
        P("wall", None, None),
    )
    return jax.shard_map(
        local,
        mesh=mesh,
        in_specs=placed,
        out_specs=(P(None, None, "wall", ("freq", "span")), P(None, ("freq", "span"))),
        check_vma=False,
    )
```

```python
import functools
import math

import jax
import jax.numpy as jnp
import numpy as np
from jax import lax
from jax.experimental import pallas as pl
from jax.experimental.pallas import tpu as pltpu
from jax.sharding import PartitionSpec as P

MESH = pl.DeviceIdType.MESH
V = 5
CY = 64
NF = 128
NB = 256
GROUP = 64
WALL = 8
LANES = 2 * V * CY
MESSAGE = 8 * V
EXT = V * CY
epsilon = 1e-06
HIGHEST = lax.Precision.HIGHEST
NT = (((1,), (1,)), ((), ()))
NN = (((1,), (0,)), ((), ()))


def split(x):
    high = x.astype(jnp.bfloat16)
    low = (x - high.astype(jnp.float32)).astype(jnp.bfloat16)
    return high, low


def product(a, b, dims):
    (ah, al), (bh, bl) = a, b
    dot = functools.partial(
        lax.dot_general, dimension_numbers=dims, preferred_element_type=jnp.float32
    )
    return dot(ah, bh) + (dot(ah, bl) + dot(al, bh))


def exact(a, b, dims=NN):
    return lax.dot_general(
        a, b, dimension_numbers=dims, precision=HIGHEST, preferred_element_type=jnp.float32
    )


def tables():
    scale = 1.0 / math.sqrt(NF * NB)
    n = np.arange(2 * NB)
    z = 4 * (n // 8) + n % 4
    d = (n // 4) % 2
    phase = 2.0 * np.pi * ((z[:, None] * np.arange(NB)[None, :]) % NB) / NB
    cos, sin = np.cos(phase), np.sin(phase)
    odd = (d == 1)[:, None]
    span = np.concatenate([np.where(odd, sin, cos), np.where(odd, cos, -sin)], axis=1)
    t, place = np.arange(GROUP), np.arange(GROUP)
    j = (place // 8 % 4) * 16 + (place % 8) * 2 + place // 32
    inverse, forward = [], []
    for r in range(2):
        phase = 2.0 * np.pi * ((t[:, None] * (2 * j + r)[None, :]) % NF) / NF
        pair = np.stack([np.cos(phase), -np.sin(phase)], axis=1) * scale
        inverse.append(pair.reshape(GROUP, 2, 2, 32))
        forward.append(pair.reshape(GROUP, 2 * GROUP).T)
    inverse = np.stack(inverse).transpose(3, 1, 0, 2, 4).reshape(2, GROUP, 2 * GROUP)
    out = []
    for table in (span, inverse, np.concatenate(forward, axis=1)):
        table = table.astype(np.float32)
        high = table.astype(jnp.bfloat16)
        low = (table - high.astype(np.float32)).astype(jnp.bfloat16)
        out += [high, low]
    return out


def kernel(
    amp_hbm, up_hbm, mask_hbm, quad_hbm, inv_hbm, lower_hbm, upper_hbm, rlow_hbm, rup_hbm, rpiv_hbm,
    th_hbm, tl_hbm, ch_hbm, cl_hbm, dh_hbm, dl_hbm,
    acc, zmat, nrecv, inner_ref, weight_ref,
    amp_ref, up_ref, mask_ref, quad_ref, inv_ref, lower_ref, upper_ref, rlow_ref, rup_ref, rpiv_ref,
    th_ref, tl_ref, ch_ref, cl_ref, dh_ref, dl_ref,
    kh, kl, send1, recv1, send2, recv2, invs, ph, pl_, su, et, mixed, eacc, pacc, mm,
    wsend, wrecv, msend, mrecv, bsend, brecv, lsend, lrecv, nsend, invb_h, invb_l,
    s1, r1, s2, r2, sw, rw, loads,
):
    f, s, w = lax.axis_index("freq"), lax.axis_index("span"), lax.axis_index("wall")
    chip, core = s // 2, s % 2
    me = core * 32 + f * 8 + chip
    barrier = pltpu.get_barrier_semaphore()

    fetch = [
        pltpu.make_async_copy(amp_hbm.at[:, v], amp_ref.at[:, v], loads.at[v]) for v in range(V)
    ]
    for src, dst in (
        (th_hbm, th_ref), (tl_hbm, tl_ref), (mask_hbm, mask_ref), (rlow_hbm, rlow_ref),
        (rup_hbm, rup_ref), (rpiv_hbm, rpiv_ref), (lower_hbm, lower_ref), (upper_hbm, upper_ref),
        (inv_hbm, inv_ref), (up_hbm, up_ref), (quad_hbm, quad_ref), (ch_hbm, ch_ref),
        (cl_hbm, cl_ref), (dh_hbm, dh_ref), (dl_hbm, dl_ref),
    ):
        fetch.append(pltpu.make_async_copy(src, dst, loads.at[len(fetch)]))
    fetch[V + 2].start()
    for copy in fetch[: V + 2] + fetch[V + 3 :]:
        copy.start()

    def peer(i):
        i = jnp.where(i >= 7, i + 1, i)
        n = 7 - i % 8
        dz = (n % 2) * ((n + 1) // 2) + (1 - n % 2) * ((8 - n // 2) % 8)
        df, dc = (i // 8) % 4, i // 32
        pf, pc, pz = (f + df) % 4, (core + dc) % 2, (chip + dz) % 8
        return {"freq": pf, "span": pz * 2 + pc}, pc * 32 + pf * 8 + pz

    def greet(i, carry):
        pl.semaphore_signal(barrier, inc=1, device_id=peer(i)[0], device_id_type=MESH)
        return carry

    lax.fori_loop(0, GROUP - 1, greet, 0)
    for i in range(1, WALL):
        pl.semaphore_signal(barrier, inc=1, device_id={"wall": (w + i) % WALL}, device_id_type=MESH)

    def tile(index):
        return pl.ds(pl.multiple_of(MESSAGE * index, 8), MESSAGE)

    def message(i, src, dst, ssem, rsem, inbound):
        device, p = peer(i)
        at = p if inbound else me
        return pltpu.make_async_remote_copy(
            src_ref=src.at[tile(p)], dst_ref=dst.at[tile(at)], send_sem=ssem.at[p],
            recv_sem=rsem.at[at], device_id=device, device_id_type=MESH,
        )

    def exchange(*args):
        def go(i, carry):
            message(i, *args, False).start()
            return carry

        lax.fori_loop(0, GROUP - 1, go, 0)

    def arrive(first, last, *args):
        def done(i, carry):
            message(i, *args, True).wait_recv()
            return carry

        lax.fori_loop(first, last, done, 0)

    def sent(*args):
        def done(i, carry):
            message(i, *args, True).wait_send()
            return carry

        lax.fori_loop(0, GROUP - 1, done, 0)

    parts = ((core, 0, 31), (1 - core, 31, GROUP - 1))

    def wall_copy(step, i, src, dst, inbound=False):
        p = (w + i) % WALL
        return pltpu.make_async_remote_copy(
            src_ref=src(p), dst_ref=dst.at[p if inbound else w], send_sem=sw.at[step, p],
            recv_sem=rw.at[step, p if inbound else w], device_id={"wall": p}, device_id_type=MESH,
        )

    fetch[V + 2].wait()
    keep = mask_ref[...].astype(jnp.float32)

    weight = jnp.zeros((1, 2 * NB), jnp.float32)
    for v in range(V):
        fetch[v].wait()
        for c in range(2):
            block = amp_ref[c, v] * keep
            weight = weight + jnp.sum(block * block, axis=0, keepdims=True)
            high, low = split(block)
            for r in range(2):
                rows = pl.ds(v * 2 * CY + r * CY, CY)
                cols = pl.ds(c * NB, NB)
                kh[rows, cols] = high[:, r * NB : (r + 1) * NB]
                kl[rows, cols] = low[:, r * NB : (r + 1) * NB]

    fetch[V].wait()
    fetch[V + 1].wait()

    def spectral(q, carry):
        rows = pl.ds(pl.multiple_of(128 * q, 128), 128)
        found = product((th_ref[rows, :], tl_ref[rows, :]), (kh[...], kl[...]), NT)
        for p in range(16):
            for v in range(V):
                at = pl.multiple_of(16 * MESSAGE * q + MESSAGE * p + 8 * v, 8)
                send1[pl.ds(at, 8), :] = found[8 * p : 8 * p + 8, 128 * v : 128 * v + 128]
        return carry

    lax.fori_loop(0, 4, spectral, 0)
    pl.semaphore_wait(barrier, GROUP - 1 + WALL - 1)
    exchange(send1, recv1, s1, r1)
    recv1[tile(me), :] = send1[tile(me), :]

    for copy in fetch[V + 3 :]:
        copy.wait()
    msend[...] = jnp.zeros_like(msend)
    msend[0:10, 0:10] = rlow_ref[:, 0]
    msend[16:26, 0:10] = rup_ref[:, 0]
    msend[32:42, 0:10] = rpiv_ref[:, 0]
    for q in range(4):
        msend[48 + q : 49 + q, :] = weight[:, 128 * q : 128 * (q + 1)]
    for i in range(1, WALL):
        wall_copy(0, i, lambda p: msend, mrecv).start()
    mrecv[w] = msend[...]

    invs[...] = jnp.zeros_like(invs)
    invs[:, 0:EXT] = inv_ref[0]
    row = lax.broadcasted_iota(jnp.int32, (16, 384), 0)
    col = lax.broadcasted_iota(jnp.int32, (16, 384), 1)
    ends = jnp.zeros((16, 384), jnp.float32)
    for v in range(V):
        for q in range(V):
            first = (row == q) & (col == v * CY)
            last = (row == V + q) & (col == v * CY + CY - 1)
            ends = jnp.where(first, lower_ref[v, :, q : q + 1], ends)
            ends = jnp.where(last, upper_ref[v, :, q : q + 1], ends)
    et[...] = ends
    zt = exact(et[...], invs[...], NT)
    zmat[...] = exact(invs[...], et[...], NT)
    for c in range(2):
        kept = (amp_ref[c] * keep).reshape(EXT, 2 * NB)
        found = exact(zt, kept)
        for q in range(4):
            wsend[q, c] = found[:, 128 * q : 128 * (q + 1)]
    for i in range(1, WALL):
        wall_copy(1, i, lambda p: wsend.at[p % 4], wrecv).start()
    wrecv[w] = wsend[w % 4]

    lower_half = lax.broadcasted_iota(jnp.int32, (EXT, 128), 1) < CY
    for v in range(V):
        here = invs[:, 128 * (v // 2) : 128 * (v // 2) + 128]
        there = pltpu.roll(here, CY, 1)
        for r in range(2):
            inside = lower_half if r == 0 else jnp.logical_not(lower_half)
            high, low = split(jnp.where(inside, here if v % 2 == r else there, 0.0))
            ph[r * EXT : (r + 1) * EXT, 128 * v : 128 * (v + 1)] = high
            pl_[r * EXT : (r + 1) * EXT, 128 * v : 128 * (v + 1)] = low
    inv_h, inv_l = split(inv_ref[0])
    for c in range(2):
        source = split(up_ref[c].reshape(EXT, 2 * NB))
        su[:, c * 2 * NB : (c + 1) * 2 * NB] = product((inv_h, inv_l), source, NN)

    for i in range(1, WALL):
        wall_copy(0, i, lambda p: msend, mrecv, True).wait()
    row = lax.broadcasted_iota(jnp.int32, (16, 128), 0)
    col = lax.broadcasted_iota(jnp.int32, (16, 128), 1)
    ahead = []
    for i in range(WALL):
        unit = jnp.where((col == 16 * i + row) & (row < 2 * V), 1.0, 0.0)
        ahead.append(unit if i == 0 else unit - exact(mrecv[i, 0:16, 0:16], ahead[-1]))
    interface = [None] * WALL
    for i in range(WALL - 1, -1, -1):
        value = ahead[i]
        if i < WALL - 1:
            value = value - exact(mrecv[i, 16:32, 0:16], interface[i + 1])
        interface[i] = exact(mrecv[i, 32:48, 0:16], value)
    for i in range(WALL):
        need = jnp.zeros((16, 128), jnp.float32)
        if i > 0:
            need = jnp.where(row < V, pltpu.roll(interface[i - 1], 16 - V, 0), need)
        if i < WALL - 1:
            need = jnp.where((row >= V) & (row < 2 * V), pltpu.roll(interface[i + 1], V, 0), need)
        mm[16 * i : 16 * (i + 1), :] = need
    total_weight = mrecv[0, 48:56, :]
    for i in range(1, WALL):
        total_weight = total_weight + mrecv[i, 48:56, :]
    weight_ref[...] = total_weight + epsilon
    invb_h[...] = jnp.zeros_like(invb_h)
    invb_l[...] = jnp.zeros_like(invb_l)
    for r in range(2):
        for e in range(2):
            for v in range(V):
                to, at = 16 * r + e * V + v, r * EXT + v * CY + e * (CY - 1)
                invb_h[to : to + 1, :] = ph[at : at + 1, :]
                invb_l[to : to + 1, :] = pl_[at : at + 1, :]
    for i in range(1, WALL):
        wall_copy(1, i, lambda p: wsend.at[p % 4], wrecv, True).wait()

    half = lax.broadcasted_iota(jnp.int32, (GROUP, 128), 1) < CY
    sign = jnp.where(half, 1.0, -1.0)
    halves = lax.broadcasted_iota(jnp.int32, (GROUP, LANES), 1) % 128 < CY
    for stage, (parity, first, last) in enumerate(parts):
        arrive(first, last, send1, recv1, s1, r1)
        for z in range(4):
            picked = jnp.concatenate([
                jnp.concatenate([
                    recv1[pl.ds(32 * MESSAGE * parity + 8 * v + 4 * d + z, 32, stride=MESSAGE), :]
                    for v in range(V)
                ], axis=1) for d in range(2)
            ], axis=0)
            stacked = jnp.concatenate(
                [jnp.where(halves, picked, 0.0), jnp.where(halves, 0.0, picked)], axis=0
            )
            found = product((ch_ref[parity], cl_ref[parity]), split(stacked), NN)
            mixed[z] = found if stage == 0 else mixed[z] + found
    pairs = [(a, b) for a in range(V) for b in range(a + 1, V)]
    weights = [[
        jnp.broadcast_to(
            quad_ref[o, a : a + 1, b : b + 1] + quad_ref[o, b : b + 1, a : a + 1], (8, 128)
        ) for a, b in pairs
    ] for o in range(V)]
    for z in range(4):
        field = []
        for v in range(V):
            x = mixed[z, :, 128 * v : 128 * (v + 1)]
            field.append((pltpu.roll(x, CY, 1) + sign * x).reshape(8, 8, 128))
        force = [jnp.zeros((8, 8, 128), jnp.float32) for _ in range(V)]
        for n, (a, b) in enumerate(pairs):
            both = field[a] * field[b]
            for o in range(V):
                force[o] = force[o] + weights[o][n][None] * both
        force = [x.reshape(GROUP, 128) for x in force]
        folded = jnp.concatenate([pltpu.roll(x, CY, 1) + sign * x for x in force], axis=1)
        stacked = jnp.concatenate(
            [jnp.where(halves, folded, 0.0), jnp.where(halves, 0.0, folded)], axis=0
        )
        back = product((dh_ref[...], dl_ref[...]), split(stacked), NN)
        for v in range(V):
            for d in range(2):
                send2[pl.ds(8 * v + 4 * d + z, GROUP, stride=MESSAGE), :] = back[
                    GROUP * d : GROUP * (d + 1), 128 * v : 128 * (v + 1)
                ]
    exchange(send2, recv2, s2, r2)
    recv2[tile(me), :] = send2[tile(me), :]

    sent(send1, recv1, s1, r1)
    for stage, (parity, first, last) in enumerate(parts):
        arrive(first, last, send2, recv2, s2, r2)
        rows = pl.ds(pl.multiple_of(32 * MESSAGE * parity, 8), 32 * MESSAGE)
        landed = recv2[rows, :].reshape(32, V, 8, 128)
        arrived = split(
            jnp.concatenate([landed[:, v].reshape(2 * 128, 128) for v in range(V)], axis=1)
        )
        rows = pl.ds(pl.multiple_of(256 * parity, 256), 256)
        table = (th_ref[rows, :], tl_ref[rows, :])
        found = product((invb_h[...], invb_l[...]), arrived, NT)
        found = product(split(found), table, NN)
        if stage == 0:
            eacc[...] = found
            found = product((ph[...], pl_[...]), arrived, NT)
            pacc[...] = product(split(found), table, NN)
    edges = eacc[...] + found
    for r in range(2):
        edge = edges[16 * r : 16 * (r + 1)]
        for c in range(2):
            for q in range(2):
                at = r * NB + q * 128
                part = edge[:, c * NB + q * 128 : c * NB + (q + 1) * 128]
                for e in range(2):
                    for v in range(V):
                        o = v * CY + e * (CY - 1)
                        bsend[c * 4 + r * 2 + q, e * V + v : e * V + v + 1, :] = (
                            part[e * V + v : e * V + v + 1, :]
                            + su[o : o + 1, c * 2 * NB + at : c * 2 * NB + at + 128]
                        ) * keep[:, at : at + 128]
    for q in range(WALL):
        bsend[q, 2 * V : 16, :] = jnp.zeros((16 - 2 * V, 128), jnp.float32)
    for i in range(1, WALL):
        wall_copy(2, i, lambda p: bsend.at[p], brecv).start()
    brecv[w] = bsend[w]

    pacc[...] += product(split(product((ph[...], pl_[...]), arrived, NT)), table, NN)
    for r in range(2):
        for c in range(2):
            at = c * 2 * NB + r * NB
            acc[:, at : at + NB] = (
                pacc[r * EXT : (r + 1) * EXT, c * NB : (c + 1) * NB] + su[:, at : at + NB]
            ) * keep[:, r * NB : (r + 1) * NB]
    real = jnp.zeros((1, 2 * NB), jnp.float32)
    imag = jnp.zeros((1, 2 * NB), jnp.float32)
    for v in range(V):
        rows = slice(v * CY, (v + 1) * CY)
        k0, k1 = amp_ref[0, v] * keep, amp_ref[1, v] * keep
        c0, c1 = acc[rows, 0 : 2 * NB] - k0, acc[rows, 2 * NB : 4 * NB] - k1
        real = real + jnp.sum(k0 * c0 + k1 * c1, axis=0, keepdims=True)
        imag = imag + jnp.sum(k0 * c1 - k1 * c0, axis=0, keepdims=True)
    for q in range(4):
        lsend[q : q + 1, :] = real[:, 128 * q : 128 * (q + 1)]
        lsend[4 + q : 5 + q, :] = imag[:, 128 * q : 128 * (q + 1)]
    for i in range(1, WALL):
        wall_copy(3, i, lambda p: lsend, lrecv).start()
    lrecv[w] = lsend[...]

    for i in range(1, WALL):
        wall_copy(2, i, lambda p: bsend.at[p], brecv, True).wait()
    need = exact(mm[...], brecv[...].reshape(16 * WALL, 128))
    part = w // 4
    same = wrecv[:, part].reshape(16 * WALL, 128)
    other = wrecv[:, 1 - part].reshape(16 * WALL, 128)
    turn = (2 * part - 1).astype(jnp.float32)
    real = jnp.sum(same * need, axis=0, keepdims=True)
    imag = jnp.sum(other * need, axis=0, keepdims=True) * turn
    nsend[...] = need.reshape(WALL, 16, 128)
    for i in range(WALL):
        nsend[i, 10:11, :] = real
        nsend[i, 11:12, :] = imag
    for i in range(1, WALL):
        wall_copy(4, i, lambda p: nsend.at[p], nrecv).start()
    nrecv[w] = nsend[w]
    for i in range(1, WALL):
        wall_copy(3, i, lambda p: lsend, lrecv, True).wait()
    inner = lrecv[0]
    for i in range(1, WALL):
        inner = inner + lrecv[i]
    inner_ref[...] = inner
    sent(send2, recv2, s2, r2)
    for i in range(1, WALL):
        wall_copy(4, i, lambda p: nsend.at[p], nrecv, True).wait()


def update(acc_ref, zmat_ref, near_ref, inner_ref, weight_ref, new_hbm, shift_ref, new, sems):
    near = split(jnp.concatenate([near_ref[q] for q in range(WALL)], axis=1))
    stores = []
    for v in range(V):
        rows = slice(v * CY, (v + 1) * CY)
        value = acc_ref[rows, :] - product(split(zmat_ref[rows, :]), near, NN)
        new[0, v] = value[:, 0 : 2 * NB]
        new[1, v] = value[:, 2 * NB : 4 * NB]
        stores.append(pltpu.make_async_copy(new.at[:, v], new_hbm.at[:, v], sems.at[v]))
        stores[-1].start()
    for q in range(4):
        real = inner_ref[q : q + 1, :] - near_ref[q, 10:11, :] - near_ref[4 + q, 10:11, :]
        imag = inner_ref[4 + q : 5 + q, :] - near_ref[q, 11:12, :] - near_ref[4 + q, 11:12, :]
        size = weight_ref[q : q + 1, :]
        shift_ref[0:1, 128 * q : 128 * (q + 1)] = imag / size
        shift_ref[1:2, 128 * q : 128 * (q + 1)] = -real / size
    for store in stores:
        store.wait()


def solution(mesh):
    consts = tables()

    def local(
        amplitudes, upstream, harmonic_mask, quadratic_coefficients, slab_inverse,
        lower_coupling, upper_coupling, reduced_lower, reduced_upper, reduced_pivot,
    ):
        vmem = pl.BlockSpec(memory_space=pltpu.VMEM)
        f32, bf16 = jnp.float32, jnp.bfloat16
        modes = amplitudes.shape[3]
        hbm = pl.BlockSpec(memory_space=pltpu.HBM)

        def turned(block):
            return jnp.transpose(block, (1, 0, 2))

        acc, zmat, near, inner, weight = pl.pallas_call(
            kernel,
            out_shape=(
                jax.ShapeDtypeStruct((EXT, 4 * NB), f32),
                jax.ShapeDtypeStruct((EXT, 16), f32),
                jax.ShapeDtypeStruct((WALL, 16, 128), f32),
                jax.ShapeDtypeStruct((8, 128), f32),
                jax.ShapeDtypeStruct((8, 128), f32),
            ),
            in_specs=[hbm] * 16,
            out_specs=(vmem,) * 5,
            scratch_shapes=[
                pltpu.VMEM((2, V, CY, 2 * NB), f32),
                pltpu.VMEM((2, V, CY, 2 * NB), f32),
                pltpu.VMEM((1, modes), jnp.int32),
                pltpu.VMEM((V, V, V), f32),
                pltpu.VMEM((1, EXT, EXT), f32),
                pltpu.VMEM((V, 1, V), f32),
                pltpu.VMEM((V, 1, V), f32),
                pltpu.VMEM((2 * V, 1, 2 * V), f32),
                pltpu.VMEM((2 * V, 1, 2 * V), f32),
                pltpu.VMEM((2 * V, 1, 2 * V), f32),
                pltpu.VMEM((2 * NB, 2 * NB), bf16),
                pltpu.VMEM((2 * NB, 2 * NB), bf16),
                pltpu.VMEM((2, GROUP, 2 * GROUP), bf16),
                pltpu.VMEM((2, GROUP, 2 * GROUP), bf16),
                pltpu.VMEM((2 * GROUP, 2 * GROUP), bf16),
                pltpu.VMEM((2 * GROUP, 2 * GROUP), bf16),
                pltpu.VMEM((LANES, 2 * NB), bf16),
                pltpu.VMEM((LANES, 2 * NB), bf16),
                pltpu.VMEM((GROUP * MESSAGE, 128), f32),
                pltpu.VMEM((GROUP * MESSAGE, 128), f32),
                pltpu.VMEM((GROUP * MESSAGE, 128), f32),
                pltpu.VMEM((GROUP * MESSAGE, 128), f32),
                pltpu.VMEM((EXT, 384), f32),
                pltpu.VMEM((2 * EXT, LANES), bf16),
                pltpu.VMEM((2 * EXT, LANES), bf16),
                pltpu.VMEM((EXT, 4 * NB), f32),
                pltpu.VMEM((16, 384), f32),
                pltpu.VMEM((4, GROUP, LANES), f32),
                pltpu.VMEM((32, 2 * NB), f32),
                pltpu.VMEM((2 * EXT, 2 * NB), f32),
                pltpu.VMEM((128, 128), f32),
                pltpu.VMEM((4, 2, 16, 128), f32),
                pltpu.VMEM((WALL, 2, 16, 128), f32),
                pltpu.VMEM((56, 128), f32),
                pltpu.VMEM((WALL, 56, 128), f32),
                pltpu.VMEM((WALL, 16, 128), f32),
                pltpu.VMEM((WALL, 16, 128), f32),
                pltpu.VMEM((8, 128), f32),
                pltpu.VMEM((WALL, 8, 128), f32),
                pltpu.VMEM((WALL, 16, 128), f32),
                pltpu.VMEM((32, LANES), bf16),
                pltpu.VMEM((32, LANES), bf16),
                pltpu.SemaphoreType.DMA((GROUP,)),
                pltpu.SemaphoreType.DMA((GROUP,)),
                pltpu.SemaphoreType.DMA((GROUP,)),
                pltpu.SemaphoreType.DMA((GROUP,)),
                pltpu.SemaphoreType.DMA((5, WALL)),
                pltpu.SemaphoreType.DMA((5, WALL)),
                pltpu.SemaphoreType.DMA((V + 15,)),
            ],
            compiler_params=pltpu.CompilerParams(
                collective_id=0, has_side_effects=True, vmem_limit_bytes=40 << 20
            ),
        )(*[pltpu.with_memory_space_constraint(x, pltpu.HBM) for x in [
            amplitudes, upstream, harmonic_mask.reshape(1, modes), quadratic_coefficients,
            slab_inverse, turned(lower_coupling), turned(upper_coupling), turned(reduced_lower),
            turned(reduced_upper), turned(reduced_pivot),
            *[jnp.asarray(table) for table in consts],
        ]])
        return pl.pallas_call(
            update,
            out_shape=(
                jax.ShapeDtypeStruct(amplitudes.shape, f32),
                jax.ShapeDtypeStruct((2, modes), f32),
            ),
            in_specs=[vmem] * 5,
            out_specs=(hbm, vmem),
            scratch_shapes=[
                pltpu.VMEM((2, V, CY, 2 * NB), f32),
                pltpu.SemaphoreType.DMA((V,)),
            ],
            compiler_params=pltpu.CompilerParams(vmem_limit_bytes=16 << 20),
        )(acc, zmat, near, inner, weight)

    placed = (
        P(None, None, "wall", ("freq", "span")),
        P(None, None, "wall", ("freq", "span")),
        P(("freq", "span")),
        P(),
        P("wall", None, None),
        P("wall", None, None),
        P("wall", None, None),
        P("wall", None, None),
        P("wall", None, None),
        P("wall", None, None),
    )
    return jax.shard_map(
        local,
        mesh=mesh,
        in_specs=placed,
        out_specs=(P(None, None, "wall", ("freq", "span")), P(None, ("freq", "span"))),
        check_vma=False,
    )
```

```python
import functools
import math

import jax
import jax.numpy as jnp
import numpy as np
from jax import lax
from jax.experimental import pallas as pl
from jax.experimental.pallas import tpu as pltpu
from jax.sharding import PartitionSpec as P

MESH = pl.DeviceIdType.MESH
V = 5
CY = 64
NF = 128
NB = 256
GROUP = 64
WALL = 8
LANES = 2 * V * CY
MESSAGE = 4 * V
PITCH = 24
EXT = V * CY
epsilon = 1e-06
HIGHEST = lax.Precision.HIGHEST
NT = (((1,), (1,)), ((), ()))
NN = (((1,), (0,)), ((), ()))


def split(x):
    high = x.astype(jnp.bfloat16)
    low = (x - high.astype(jnp.float32)).astype(jnp.bfloat16)
    return high, low


def product(a, b, dims):
    (ah, al), (bh, bl) = a, b
    dot = functools.partial(
        lax.dot_general, dimension_numbers=dims, preferred_element_type=jnp.float32
    )
    return dot(ah, bh) + (dot(ah, bl) + dot(al, bh))


def exact(a, b, dims=NN):
    return lax.dot_general(
        a, b, dimension_numbers=dims, precision=HIGHEST, preferred_element_type=jnp.float32
    )


def tables():
    scale = 1.0 / math.sqrt(NF * NB)
    n = np.arange(2 * NB)
    z = 4 * (n // 4 % GROUP) + 2 * (n // (4 * GROUP)) + n % 2
    d = (n // 2) % 2
    phase = 2.0 * np.pi * ((z[:, None] * np.arange(NB)[None, :]) % NB) / NB
    cos, sin = np.cos(phase), np.sin(phase)
    odd = (d == 1)[:, None]
    span = np.concatenate([np.where(odd, sin, cos), np.where(odd, cos, -sin)], axis=1)
    t, place = np.arange(GROUP), np.arange(GROUP)
    j = (place // 8 % 4) * 16 + (place % 8) * 2 + place // 32
    inverse, forward = [], []
    for r in range(2):
        phase = 2.0 * np.pi * ((t[:, None] * (2 * j + r)[None, :]) % NF) / NF
        pair = np.stack([np.cos(phase), -np.sin(phase)], axis=1) * scale
        inverse.append(pair.reshape(GROUP, 2 * GROUP))
        forward.append(pair.reshape(GROUP, 2 * GROUP).T)
    out = []
    for table in (span, np.concatenate(inverse, axis=1), np.concatenate(forward, axis=1)):
        table = table.astype(np.float32)
        high = table.astype(jnp.bfloat16)
        low = (table - high.astype(np.float32)).astype(jnp.bfloat16)
        out += [high, low]
    return out


def kernel(
    amp_hbm, up_hbm, mask_hbm, quad_hbm, inv_hbm, lower_hbm, upper_hbm, rlow_hbm, rup_hbm, rpiv_hbm,
    th_hbm, tl_hbm, ch_hbm, cl_hbm, dh_hbm, dl_hbm,
    acc, zmat, nrecv, inner_ref, weight_ref,
    amp_ref, up_ref, mask_ref, quad_ref, inv_ref, lower_ref, upper_ref, rlow_ref, rup_ref, rpiv_ref,
    th_ref, tl_ref, ch_ref, cl_ref, dh_ref, dl_ref,
    kh, kl, send1, recv1, send2, recv2, invs, ph, pl_, su, et, eacc, pacc, mm,
    wsend, wrecv, msend, mrecv, bsend, brecv, lsend, lrecv, nsend, invb_h, invb_l,
    s1, r1, s2, r2, sw, rw, loads,
):
    f, s, w = lax.axis_index("freq"), lax.axis_index("span"), lax.axis_index("wall")
    chip, core = s // 2, s % 2
    me = core * 32 + f * 8 + chip
    barrier = pltpu.get_barrier_semaphore()

    fetch = [
        pltpu.make_async_copy(amp_hbm.at[:, v], amp_ref.at[:, v], loads.at[v]) for v in range(V)
    ]
    for src, dst in (
        (th_hbm, th_ref), (tl_hbm, tl_ref), (mask_hbm, mask_ref), (rlow_hbm, rlow_ref),
        (rup_hbm, rup_ref), (rpiv_hbm, rpiv_ref), (lower_hbm, lower_ref), (upper_hbm, upper_ref),
        (inv_hbm, inv_ref), (up_hbm, up_ref), (quad_hbm, quad_ref), (ch_hbm, ch_ref),
        (cl_hbm, cl_ref), (dh_hbm, dh_ref), (dl_hbm, dl_ref),
    ):
        fetch.append(pltpu.make_async_copy(src, dst, loads.at[len(fetch)]))
    fetch[V + 2].start()
    for copy in fetch[: V + 2] + fetch[V + 3 :]:
        copy.start()

    def peer(i):
        i = jnp.where(i >= 7, i + 1, i)
        n = 7 - i % 8
        dz = (n % 2) * ((n + 1) // 2) + (1 - n % 2) * ((8 - n // 2) % 8)
        df, dc = (i // 8) % 4, i // 32
        pf, pc, pz = (f + df) % 4, (core + dc) % 2, (chip + dz) % 8
        return {"freq": pf, "span": pz * 2 + pc}, pc * 32 + pf * 8 + pz

    def greet(i, carry):
        pl.semaphore_signal(barrier, inc=1, device_id=peer(i)[0], device_id_type=MESH)
        return carry

    lax.fori_loop(0, GROUP - 1, greet, 0)
    for i in range(1, WALL):
        pl.semaphore_signal(barrier, inc=1, device_id={"wall": (w + i) % WALL}, device_id_type=MESH)

    def flat(half, index):
        return pl.ds(pl.multiple_of(PITCH * (GROUP * half + index), 8), MESSAGE)

    def paired(half, index):
        return GROUP // 2 * half + index // 2, index % 2, pl.ds(0, MESSAGE)

    def message(half, i, src, dst, src_at, dst_at, ssem, rsem, inbound):
        device, p = peer(i)
        at = p if inbound else me
        return pltpu.make_async_remote_copy(
            src_ref=src.at[src_at(half, p)], dst_ref=dst.at[dst_at(half, at)],
            send_sem=ssem.at[half, p], recv_sem=rsem.at[half, at], device_id=device,
            device_id_type=MESH,
        )

    out = (send1, recv1, paired, flat, s1, r1)
    back = (send2, recv2, flat, paired, s2, r2)

    def exchange(half, args):
        def go(i, carry):
            message(half, i, *args, False).start()
            return carry

        lax.fori_loop(0, GROUP - 1, go, 0)

    def arrive(half, args):
        def done(i, carry):
            message(half, i, *args, True).wait_recv()
            return carry

        lax.fori_loop(0, GROUP - 1, done, 0)

    def sent(args):
        def done(i, carry):
            for half in range(2):
                message(half, i, *args, True).wait_send()
            return carry

        lax.fori_loop(0, GROUP - 1, done, 0)

    def wall_copy(step, i, src, dst, inbound=False):
        p = (w + i) % WALL
        return pltpu.make_async_remote_copy(
            src_ref=src(p), dst_ref=dst.at[p if inbound else w], send_sem=sw.at[step, p],
            recv_sem=rw.at[step, p if inbound else w], device_id={"wall": p}, device_id_type=MESH,
        )

    fetch[V + 2].wait()
    keep = mask_ref[...].astype(jnp.float32)

    weight = jnp.zeros((1, 2 * NB), jnp.float32)
    for v in range(V):
        fetch[v].wait()
        for c in range(2):
            block = amp_ref[c, v] * keep
            weight = weight + jnp.sum(block * block, axis=0, keepdims=True)
            high, low = split(block)
            for r in range(2):
                rows = pl.ds(v * 2 * CY + r * CY, CY)
                cols = pl.ds(c * NB, NB)
                kh[rows, cols] = high[:, r * NB : (r + 1) * NB]
                kl[rows, cols] = low[:, r * NB : (r + 1) * NB]

    fetch[V].wait()
    fetch[V + 1].wait()

    upper_rows = lax.broadcasted_iota(jnp.int32, (16, 8, 128), 1) >= 4

    def turn_rows(x):
        return pltpu.roll(x, 4, 1)

    def join(first, second, parity):
        if parity == 0:
            return jnp.where(upper_rows, turn_rows(second), first)
        return jnp.where(upper_rows, second, turn_rows(first))

    def spectral(q, carry):
        rows = pl.ds(pl.multiple_of(128 * q, 128), 128)
        found = product((th_ref[rows, :], tl_ref[rows, :]), (kh[...], kl[...]), NT)
        tiles = [found[:, 128 * v : 128 * (v + 1)].reshape(16, 8, 128) for v in range(V)]
        at = pl.ds(pl.multiple_of(16 * q, 16), 16)
        for parity in range(2):
            for n in range(2):
                send1[at, parity, 8 * n : 8 * n + 8] = join(
                    tiles[2 * n], tiles[2 * n + 1], parity
                )
            send1[at, parity, 16:24] = turn_rows(tiles[4]) if parity else tiles[4]
        return carry

    lax.fori_loop(0, 2, spectral, 0)
    pl.semaphore_wait(barrier, GROUP - 1 + WALL - 1)
    exchange(0, out)
    lax.fori_loop(2, 4, spectral, 0)
    exchange(1, out)
    for half in range(2):
        recv1[flat(half, me), :] = send1[paired(half, me)]

    for copy in fetch[V + 3 :]:
        copy.wait()
    msend[...] = jnp.zeros_like(msend)
    msend[0:10, 0:10] = rlow_ref[:, 0]
    msend[16:26, 0:10] = rup_ref[:, 0]
    msend[32:42, 0:10] = rpiv_ref[:, 0]
    for q in range(4):
        msend[48 + q : 49 + q, :] = weight[:, 128 * q : 128 * (q + 1)]
    for i in range(1, WALL):
        wall_copy(0, i, lambda p: msend, mrecv).start()
    mrecv[w] = msend[...]

    invs[...] = jnp.zeros_like(invs)
    invs[:, 0:EXT] = inv_ref[0]
    row = lax.broadcasted_iota(jnp.int32, (16, 384), 0)
    col = lax.broadcasted_iota(jnp.int32, (16, 384), 1)
    ends = jnp.zeros((16, 384), jnp.float32)
    for v in range(V):
        for q in range(V):
            first = (row == q) & (col == v * CY)
            last = (row == V + q) & (col == v * CY + CY - 1)
            ends = jnp.where(first, lower_ref[v, :, q : q + 1], ends)
            ends = jnp.where(last, upper_ref[v, :, q : q + 1], ends)
    et[...] = ends
    zt = exact(et[...], invs[...], NT)
    zmat[...] = exact(invs[...], et[...], NT)
    for c in range(2):
        kept = (amp_ref[c] * keep).reshape(EXT, 2 * NB)
        found = exact(zt, kept)
        for q in range(4):
            wsend[q, c] = found[:, 128 * q : 128 * (q + 1)]
    for i in range(1, WALL):
        wall_copy(1, i, lambda p: wsend.at[p % 4], wrecv).start()
    wrecv[w] = wsend[w % 4]

    lower_half = lax.broadcasted_iota(jnp.int32, (EXT, 128), 1) < CY
    for v in range(V):
        here = invs[:, 128 * (v // 2) : 128 * (v // 2) + 128]
        there = pltpu.roll(here, CY, 1)
        for r in range(2):
            inside = lower_half if r == 0 else jnp.logical_not(lower_half)
            high, low = split(jnp.where(inside, here if v % 2 == r else there, 0.0))
            ph[r * EXT : (r + 1) * EXT, 128 * v : 128 * (v + 1)] = high
            pl_[r * EXT : (r + 1) * EXT, 128 * v : 128 * (v + 1)] = low
    inv_h, inv_l = split(inv_ref[0])
    for c in range(2):
        source = split(up_ref[c].reshape(EXT, 2 * NB))
        su[:, c * 2 * NB : (c + 1) * 2 * NB] = product((inv_h, inv_l), source, NN)

    for i in range(1, WALL):
        wall_copy(0, i, lambda p: msend, mrecv, True).wait()
    row = lax.broadcasted_iota(jnp.int32, (16, 128), 0)
    col = lax.broadcasted_iota(jnp.int32, (16, 128), 1)
    ahead = []
    for i in range(WALL):
        unit = jnp.where((col == 16 * i + row) & (row < 2 * V), 1.0, 0.0)
        ahead.append(unit if i == 0 else unit - exact(mrecv[i, 0:16, 0:16], ahead[-1]))
    interface = [None] * WALL
    for i in range(WALL - 1, -1, -1):
        value = ahead[i]
        if i < WALL - 1:
            value = value - exact(mrecv[i, 16:32, 0:16], interface[i + 1])
        interface[i] = exact(mrecv[i, 32:48, 0:16], value)
    for i in range(WALL):
        need = jnp.zeros((16, 128), jnp.float32)
        if i > 0:
            need = jnp.where(row < V, pltpu.roll(interface[i - 1], 16 - V, 0), need)
        if i < WALL - 1:
            need = jnp.where((row >= V) & (row < 2 * V), pltpu.roll(interface[i + 1], V, 0), need)
        mm[16 * i : 16 * (i + 1), :] = need
    total_weight = mrecv[0, 48:56, :]
    for i in range(1, WALL):
        total_weight = total_weight + mrecv[i, 48:56, :]
    weight_ref[...] = total_weight + epsilon
    invb_h[...] = jnp.zeros_like(invb_h)
    invb_l[...] = jnp.zeros_like(invb_l)
    for r in range(2):
        for e in range(2):
            for v in range(V):
                to, at = 16 * r + e * V + v, r * EXT + v * CY + e * (CY - 1)
                invb_h[to : to + 1, :] = ph[at : at + 1, :]
                invb_l[to : to + 1, :] = pl_[at : at + 1, :]
    for i in range(1, WALL):
        wall_copy(1, i, lambda p: wsend.at[p % 4], wrecv, True).wait()

    half = lax.broadcasted_iota(jnp.int32, (GROUP, 128), 1) < CY
    sign = jnp.where(half, 1.0, -1.0)
    wide = lax.broadcasted_iota(jnp.int32, (128, LANES), 1) % 128 < CY
    halves = lax.broadcasted_iota(jnp.int32, (GROUP, LANES), 1) % 128 < CY
    pairs = [(a, b) for a in range(V) for b in range(a + 1, V)]
    weights = [[
        jnp.broadcast_to(
            quad_ref[o, a : a + 1, b : b + 1] + quad_ref[o, b : b + 1, a : a + 1], (8, 128)
        ) for a, b in pairs
    ] for o in range(V)]
    def point(half, z):
        start = PITCH * GROUP * half + z
        picked = jnp.concatenate([
            jnp.concatenate([
                recv1[pl.ds(start + 4 * v + 2 * d, GROUP, stride=PITCH), :] for v in range(V)
            ], axis=1) for d in range(2)
        ], axis=0)
        stacked = jnp.concatenate(
            [jnp.where(wide, picked, 0.0), jnp.where(wide, 0.0, picked)], axis=0
        )
        mixed = product((ch_ref[...], cl_ref[...]), split(stacked), NN)
        field = []
        for v in range(V):
            x = mixed[:, 128 * v : 128 * (v + 1)]
            field.append((pltpu.roll(x, CY, 1) + sign * x).reshape(8, 8, 128))
        force = [jnp.zeros((8, 8, 128), jnp.float32) for _ in range(V)]
        for n, (a, b) in enumerate(pairs):
            both = field[a] * field[b]
            for o in range(V):
                force[o] = force[o] + weights[o][n][None] * both
        force = [x.reshape(GROUP, 128) for x in force]
        folded = jnp.concatenate([pltpu.roll(x, CY, 1) + sign * x for x in force], axis=1)
        stacked = jnp.concatenate(
            [jnp.where(halves, folded, 0.0), jnp.where(halves, 0.0, folded)], axis=0
        )
        found = product((dh_ref[...], dl_ref[...]), split(stacked), NN)
        for v in range(V):
            for d in range(2):
                send2[pl.ds(start + 4 * v + 2 * d, GROUP, stride=PITCH), :] = found[
                    GROUP * d : GROUP * (d + 1), 128 * v : 128 * (v + 1)
                ]

    for half in range(2):
        arrive(half, out)
        for z in range(2):
            point(half, z)
        exchange(half, back)
        recv2[paired(half, me)] = send2[flat(half, me), :]

    sent(out)
    upper_rows = lax.broadcasted_iota(jnp.int32, (32, 8, 128), 1) >= 4
    for half in range(2):
        arrive(half, back)
        even, odd = recv2[32 * half : 32 * half + 32, 0], recv2[32 * half : 32 * half + 32, 1]
        tiles = []
        for v in range(V):
            near, far = (x[:, 8 * (v // 2) : 8 * (v // 2) + 8] for x in (even, odd))
            if v % 2 == 0:
                tiles.append(jnp.where(upper_rows, turn_rows(far), near))
            else:
                tiles.append(jnp.where(upper_rows, far, turn_rows(near)))
        arrived = split(jnp.concatenate([x.reshape(256, 128) for x in tiles], axis=1))
        rows = pl.ds(256 * half, 256)
        table = (th_ref[rows, :], tl_ref[rows, :])
        found = product((invb_h[...], invb_l[...]), arrived, NT)
        found = product(split(found), table, NN)
        if half == 0:
            eacc[...] = found
            found = product((ph[...], pl_[...]), arrived, NT)
            pacc[...] = product(split(found), table, NN)
    edges = eacc[...] + found
    for r in range(2):
        edge = edges[16 * r : 16 * (r + 1)]
        for c in range(2):
            for q in range(2):
                at = r * NB + q * 128
                part = edge[:, c * NB + q * 128 : c * NB + (q + 1) * 128]
                for e in range(2):
                    for v in range(V):
                        o = v * CY + e * (CY - 1)
                        bsend[c * 4 + r * 2 + q, e * V + v : e * V + v + 1, :] = (
                            part[e * V + v : e * V + v + 1, :]
                            + su[o : o + 1, c * 2 * NB + at : c * 2 * NB + at + 128]
                        ) * keep[:, at : at + 128]
    for q in range(WALL):
        bsend[q, 2 * V : 16, :] = jnp.zeros((16 - 2 * V, 128), jnp.float32)
    for i in range(1, WALL):
        wall_copy(2, i, lambda p: bsend.at[p], brecv).start()
    brecv[w] = bsend[w]

    pacc[...] += product(split(product((ph[...], pl_[...]), arrived, NT)), table, NN)
    for r in range(2):
        for c in range(2):
            at = c * 2 * NB + r * NB
            acc[:, at : at + NB] = (
                pacc[r * EXT : (r + 1) * EXT, c * NB : (c + 1) * NB] + su[:, at : at + NB]
            ) * keep[:, r * NB : (r + 1) * NB]
    real = jnp.zeros((1, 2 * NB), jnp.float32)
    imag = jnp.zeros((1, 2 * NB), jnp.float32)
    for v in range(V):
        rows = slice(v * CY, (v + 1) * CY)
        k0, k1 = amp_ref[0, v] * keep, amp_ref[1, v] * keep
        c0, c1 = acc[rows, 0 : 2 * NB] - k0, acc[rows, 2 * NB : 4 * NB] - k1
        real = real + jnp.sum(k0 * c0 + k1 * c1, axis=0, keepdims=True)
        imag = imag + jnp.sum(k0 * c1 - k1 * c0, axis=0, keepdims=True)
    for q in range(4):
        lsend[q : q + 1, :] = real[:, 128 * q : 128 * (q + 1)]
        lsend[4 + q : 5 + q, :] = imag[:, 128 * q : 128 * (q + 1)]
    for i in range(1, WALL):
        wall_copy(3, i, lambda p: lsend, lrecv).start()
    lrecv[w] = lsend[...]

    for i in range(1, WALL):
        wall_copy(2, i, lambda p: bsend.at[p], brecv, True).wait()
    need = exact(mm[...], brecv[...].reshape(16 * WALL, 128))
    part = w // 4
    same = wrecv[:, part].reshape(16 * WALL, 128)
    other = wrecv[:, 1 - part].reshape(16 * WALL, 128)
    turn = (2 * part - 1).astype(jnp.float32)
    real = jnp.sum(same * need, axis=0, keepdims=True)
    imag = jnp.sum(other * need, axis=0, keepdims=True) * turn
    nsend[...] = need.reshape(WALL, 16, 128)
    for i in range(WALL):
        nsend[i, 10:11, :] = real
        nsend[i, 11:12, :] = imag
    for i in range(1, WALL):
        wall_copy(4, i, lambda p: nsend.at[p], nrecv).start()
    nrecv[w] = nsend[w]
    for i in range(1, WALL):
        wall_copy(3, i, lambda p: lsend, lrecv, True).wait()
    inner = lrecv[0]
    for i in range(1, WALL):
        inner = inner + lrecv[i]
    inner_ref[...] = inner
    sent(back)
    for i in range(1, WALL):
        wall_copy(4, i, lambda p: nsend.at[p], nrecv, True).wait()


def update(acc_ref, zmat_ref, near_ref, inner_ref, weight_ref, new_hbm, shift_ref, new, sems):
    near = split(jnp.concatenate([near_ref[q] for q in range(WALL)], axis=1))
    stores = []
    for v in range(V):
        rows = slice(v * CY, (v + 1) * CY)
        value = acc_ref[rows, :] - product(split(zmat_ref[rows, :]), near, NN)
        new[0, v] = value[:, 0 : 2 * NB]
        new[1, v] = value[:, 2 * NB : 4 * NB]
        stores.append(pltpu.make_async_copy(new.at[:, v], new_hbm.at[:, v], sems.at[v]))
        stores[-1].start()
    for q in range(4):
        real = inner_ref[q : q + 1, :] - near_ref[q, 10:11, :] - near_ref[4 + q, 10:11, :]
        imag = inner_ref[4 + q : 5 + q, :] - near_ref[q, 11:12, :] - near_ref[4 + q, 11:12, :]
        size = weight_ref[q : q + 1, :]
        shift_ref[0:1, 128 * q : 128 * (q + 1)] = imag / size
        shift_ref[1:2, 128 * q : 128 * (q + 1)] = -real / size
    for store in stores:
        store.wait()


def solution(mesh):
    consts = tables()

    def local(
        amplitudes, upstream, harmonic_mask, quadratic_coefficients, slab_inverse,
        lower_coupling, upper_coupling, reduced_lower, reduced_upper, reduced_pivot,
    ):
        vmem = pl.BlockSpec(memory_space=pltpu.VMEM)
        f32, bf16 = jnp.float32, jnp.bfloat16
        modes = amplitudes.shape[3]
        hbm = pl.BlockSpec(memory_space=pltpu.HBM)

        def turned(block):
            return jnp.transpose(block, (1, 0, 2))

        acc, zmat, near, inner, weight = pl.pallas_call(
            kernel,
            out_shape=(
                jax.ShapeDtypeStruct((EXT, 4 * NB), f32),
                jax.ShapeDtypeStruct((EXT, 16), f32),
                jax.ShapeDtypeStruct((WALL, 16, 128), f32),
                jax.ShapeDtypeStruct((8, 128), f32),
                jax.ShapeDtypeStruct((8, 128), f32),
            ),
            in_specs=[hbm] * 16,
            out_specs=(vmem,) * 5,
            scratch_shapes=[
                pltpu.VMEM((2, V, CY, 2 * NB), f32),
                pltpu.VMEM((2, V, CY, 2 * NB), f32),
                pltpu.VMEM((1, modes), jnp.int32),
                pltpu.VMEM((V, V, V), f32),
                pltpu.VMEM((1, EXT, EXT), f32),
                pltpu.VMEM((V, 1, V), f32),
                pltpu.VMEM((V, 1, V), f32),
                pltpu.VMEM((2 * V, 1, 2 * V), f32),
                pltpu.VMEM((2 * V, 1, 2 * V), f32),
                pltpu.VMEM((2 * V, 1, 2 * V), f32),
                pltpu.VMEM((2 * NB, 2 * NB), bf16),
                pltpu.VMEM((2 * NB, 2 * NB), bf16),
                pltpu.VMEM((GROUP, 4 * GROUP), bf16),
                pltpu.VMEM((GROUP, 4 * GROUP), bf16),
                pltpu.VMEM((2 * GROUP, 2 * GROUP), bf16),
                pltpu.VMEM((2 * GROUP, 2 * GROUP), bf16),
                pltpu.VMEM((LANES, 2 * NB), bf16),
                pltpu.VMEM((LANES, 2 * NB), bf16),
                pltpu.VMEM((GROUP, 2, PITCH, 128), f32),
                pltpu.VMEM((2 * GROUP * PITCH, 128), f32),
                pltpu.VMEM((2 * GROUP * PITCH, 128), f32),
                pltpu.VMEM((GROUP, 2, PITCH, 128), f32),
                pltpu.VMEM((EXT, 384), f32),
                pltpu.VMEM((2 * EXT, LANES), bf16),
                pltpu.VMEM((2 * EXT, LANES), bf16),
                pltpu.VMEM((EXT, 4 * NB), f32),
                pltpu.VMEM((16, 384), f32),
                pltpu.VMEM((32, 2 * NB), f32),
                pltpu.VMEM((2 * EXT, 2 * NB), f32),
                pltpu.VMEM((128, 128), f32),
                pltpu.VMEM((4, 2, 16, 128), f32),
                pltpu.VMEM((WALL, 2, 16, 128), f32),
                pltpu.VMEM((56, 128), f32),
                pltpu.VMEM((WALL, 56, 128), f32),
                pltpu.VMEM((WALL, 16, 128), f32),
                pltpu.VMEM((WALL, 16, 128), f32),
                pltpu.VMEM((8, 128), f32),
                pltpu.VMEM((WALL, 8, 128), f32),
                pltpu.VMEM((WALL, 16, 128), f32),
                pltpu.VMEM((32, LANES), bf16),
                pltpu.VMEM((32, LANES), bf16),
                pltpu.SemaphoreType.DMA((2, GROUP)),
                pltpu.SemaphoreType.DMA((2, GROUP)),
                pltpu.SemaphoreType.DMA((2, GROUP)),
                pltpu.SemaphoreType.DMA((2, GROUP)),
                pltpu.SemaphoreType.DMA((5, WALL)),
                pltpu.SemaphoreType.DMA((5, WALL)),
                pltpu.SemaphoreType.DMA((V + 15,)),
            ],
            compiler_params=pltpu.CompilerParams(
                collective_id=0, has_side_effects=True, vmem_limit_bytes=40 << 20
            ),
        )(*[pltpu.with_memory_space_constraint(x, pltpu.HBM) for x in [
            amplitudes, upstream, harmonic_mask.reshape(1, modes), quadratic_coefficients,
            slab_inverse, turned(lower_coupling), turned(upper_coupling), turned(reduced_lower),
            turned(reduced_upper), turned(reduced_pivot),
            *[jnp.asarray(table) for table in consts],
        ]])
        return pl.pallas_call(
            update,
            out_shape=(
                jax.ShapeDtypeStruct(amplitudes.shape, f32),
                jax.ShapeDtypeStruct((2, modes), f32),
            ),
            in_specs=[vmem] * 5,
            out_specs=(hbm, vmem),
            scratch_shapes=[
                pltpu.VMEM((2, V, CY, 2 * NB), f32),
                pltpu.SemaphoreType.DMA((V,)),
            ],
            compiler_params=pltpu.CompilerParams(vmem_limit_bytes=16 << 20),
        )(acc, zmat, near, inner, weight)

    placed = (
        P(None, None, "wall", ("freq", "span")),
        P(None, None, "wall", ("freq", "span")),
        P(("freq", "span")),
        P(),
        P("wall", None, None),
        P("wall", None, None),
        P("wall", None, None),
        P("wall", None, None),
        P("wall", None, None),
        P("wall", None, None),
    )
    return jax.shard_map(
        local,
        mesh=mesh,
        in_specs=placed,
        out_specs=(P(None, None, "wall", ("freq", "span")), P(None, ("freq", "span"))),
        check_vma=False,
    )
```

```python
import functools
import math

import jax
import jax.numpy as jnp
import numpy as np
from jax import lax
from jax.experimental import pallas as pl
from jax.experimental.pallas import tpu as pltpu
from jax.sharding import PartitionSpec as P

MESH = pl.DeviceIdType.MESH
V = 5
CY = 64
NF = 128
NB = 256
GROUP = 64
WALL = 8
LANES = 2 * V * CY
MESSAGE = 4 * V
PITCH = 24
EXT = V * CY
epsilon = 1e-06
HIGHEST = lax.Precision.HIGHEST
NT = (((1,), (1,)), ((), ()))
NN = (((1,), (0,)), ((), ()))


def split(x):
    high = x.astype(jnp.bfloat16)
    low = (x - high.astype(jnp.float32)).astype(jnp.bfloat16)
    return high, low


def product(a, b, dims):
    (ah, al), (bh, bl) = a, b
    dot = functools.partial(
        lax.dot_general, dimension_numbers=dims, preferred_element_type=jnp.float32
    )
    return dot(ah, bh) + (dot(ah, bl) + dot(al, bh))


def exact(a, b, dims=NN):
    return lax.dot_general(
        a, b, dimension_numbers=dims, precision=HIGHEST, preferred_element_type=jnp.float32
    )


def tables():
    scale = 1.0 / math.sqrt(NF * NB)
    n = np.arange(2 * NB)
    z = 4 * (n // 4 % GROUP) + 2 * (n // (4 * GROUP)) + n % 2
    d = (n // 2) % 2
    phase = 2.0 * np.pi * ((z[:, None] * np.arange(NB)[None, :]) % NB) / NB
    cos, sin = np.cos(phase), np.sin(phase)
    odd = (d == 1)[:, None]
    span = np.concatenate([np.where(odd, sin, cos), np.where(odd, cos, -sin)], axis=1)
    t, place = np.arange(GROUP), np.arange(GROUP)
    j = (place // 8 % 4) * 16 + (place % 8) * 2 + place // 32
    inverse, forward = [], []
    for r in range(2):
        phase = 2.0 * np.pi * ((t[:, None] * (2 * j + r)[None, :]) % NF) / NF
        pair = np.stack([np.cos(phase), -np.sin(phase)], axis=1) * scale
        inverse.append(pair.reshape(GROUP, 2 * GROUP))
        forward.append(pair.reshape(GROUP, 2 * GROUP).T)
    out = []
    for table in (span, np.concatenate(inverse, axis=1), np.concatenate(forward, axis=1)):
        table = table.astype(np.float32)
        high = table.astype(jnp.bfloat16)
        low = (table - high.astype(np.float32)).astype(jnp.bfloat16)
        out += [high, low]
    return out


def kernel(
    amp_hbm, up_hbm, mask_hbm, quad_hbm, inv_hbm, lower_hbm, upper_hbm, rlow_hbm, rup_hbm, rpiv_hbm,
    th_hbm, tl_hbm, ch_hbm, cl_hbm, dh_hbm, dl_hbm,
    acc, zmat, nrecv, inner_ref, weight_ref,
    amp_ref, up_ref, mask_ref, quad_ref, inv_ref, lower_ref, upper_ref, rlow_ref, rup_ref, rpiv_ref,
    th_ref, tl_ref, ch_ref, cl_ref, dh_ref, dl_ref,
    kh, kl, send1, recv1, send2, recv2, invs, ph, pl_, su, et, eacc, esource, ekeep, pacc, mm,
    wsend, wrecv, msend, mrecv, bsend, brecv, lsend, lrecv, nsend, invb_h, invb_l,
    s1, r1, s2, r2, sw, rw, loads,
):
    f, s, w = lax.axis_index("freq"), lax.axis_index("span"), lax.axis_index("wall")
    chip, core = s // 2, s % 2
    me = core * 32 + f * 8 + chip
    barrier = pltpu.get_barrier_semaphore()

    fetch = [
        pltpu.make_async_copy(amp_hbm.at[:, v], amp_ref.at[:, v], loads.at[v]) for v in range(V)
    ]
    for src, dst in (
        (th_hbm, th_ref), (tl_hbm, tl_ref), (mask_hbm, mask_ref), (rlow_hbm, rlow_ref),
        (rup_hbm, rup_ref), (rpiv_hbm, rpiv_ref), (lower_hbm, lower_ref), (upper_hbm, upper_ref),
        (inv_hbm, inv_ref), (up_hbm, up_ref), (quad_hbm, quad_ref), (ch_hbm, ch_ref),
        (cl_hbm, cl_ref), (dh_hbm, dh_ref), (dl_hbm, dl_ref),
    ):
        fetch.append(pltpu.make_async_copy(src, dst, loads.at[len(fetch)]))
    fetch[V + 2].start()
    for copy in fetch[: V + 2] + fetch[V + 3 :]:
        copy.start()

    spot = f * 8 + chip

    def everyone(act):
        for other in range(2):
            c = core if other == 0 else 1 - core

            def one(i, carry):
                p = lax.rem(spot + i, 32)
                act({"freq": lax.div(p, 8), "span": 2 * lax.rem(p, 8) + c}, 32 * c + p)
                return carry

            lax.fori_loop(1 - other, 32, one, 0)

    everyone(
        lambda device, p: pl.semaphore_signal(barrier, inc=1, device_id=device, device_id_type=MESH)
    )
    for i in range(1, WALL):
        pl.semaphore_signal(barrier, inc=1, device_id={"wall": (w + i) % WALL}, device_id_type=MESH)

    def flat(half, index):
        return pl.ds(pl.multiple_of(PITCH * (GROUP * half + index), 8), MESSAGE)

    def paired(half, index):
        return GROUP // 2 * half + lax.div(index, 2), lax.rem(index, 2), pl.ds(0, MESSAGE)

    def message(half, device, p, at, src, dst, src_at, dst_at, ssem, rsem):
        return pltpu.make_async_remote_copy(
            src_ref=src.at[src_at(half, p)], dst_ref=dst.at[dst_at(half, at)],
            send_sem=ssem.at[half, p], recv_sem=rsem.at[half, at], device_id=device,
            device_id_type=MESH,
        )

    out = (send1, recv1, paired, flat, s1, r1)
    back = (send2, recv2, flat, paired, s2, r2)

    def exchange(half, args):
        everyone(lambda device, p: message(half, device, p, me, *args).start())

    def arrive(half, args):
        everyone(lambda device, p: message(half, device, p, p, *args).wait_recv())

    def sent(args):
        for half in range(2):
            everyone(lambda device, p: message(half, device, p, p, *args).wait_send())

    def wall_copy(step, i, src, dst, inbound=False):
        p = (w + i) % WALL
        return pltpu.make_async_remote_copy(
            src_ref=src(p), dst_ref=dst.at[p if inbound else w], send_sem=sw.at[step, p],
            recv_sem=rw.at[step, p if inbound else w], device_id={"wall": p}, device_id_type=MESH,
        )

    fetch[V + 2].wait()
    keep = mask_ref[...].astype(jnp.float32)

    weight = jnp.zeros((1, 2 * NB), jnp.float32)
    for v in range(V):
        fetch[v].wait()
        for c in range(2):
            block = amp_ref[c, v] * keep
            weight = weight + jnp.sum(block * block, axis=0, keepdims=True)
            high, low = split(block)
            for r in range(2):
                rows = pl.ds(v * 2 * CY + r * CY, CY)
                cols = pl.ds(c * NB, NB)
                kh[rows, cols] = high[:, r * NB : (r + 1) * NB]
                kl[rows, cols] = low[:, r * NB : (r + 1) * NB]

    fetch[V].wait()
    fetch[V + 1].wait()

    upper_rows = lax.broadcasted_iota(jnp.int32, (16, 8, 128), 1) >= 4

    def turn_rows(x):
        return pltpu.roll(x, 4, 1)

    def join(first, second, parity):
        if parity == 0:
            return jnp.where(upper_rows, turn_rows(second), first)
        return jnp.where(upper_rows, second, turn_rows(first))

    def spectral(q, carry):
        rows = pl.ds(pl.multiple_of(128 * q, 128), 128)
        found = product((th_ref[rows, :], tl_ref[rows, :]), (kh[...], kl[...]), NT)
        tiles = [found[:, 128 * v : 128 * (v + 1)].reshape(16, 8, 128) for v in range(V)]
        at = pl.ds(pl.multiple_of(16 * q, 16), 16)
        for parity in range(2):
            for n in range(2):
                send1[at, parity, 8 * n : 8 * n + 8] = join(
                    tiles[2 * n], tiles[2 * n + 1], parity
                )
            send1[at, parity, 16:24] = turn_rows(tiles[4]) if parity else tiles[4]
        return carry

    lax.fori_loop(0, 2, spectral, 0)
    pl.semaphore_wait(barrier, GROUP - 1 + WALL - 1)
    exchange(0, out)
    lax.fori_loop(2, 4, spectral, 0)
    exchange(1, out)
    for half in range(2):
        recv1[flat(half, me), :] = send1[paired(half, me)]

    for copy in fetch[V + 3 :]:
        copy.wait()
    msend[...] = jnp.zeros_like(msend)
    msend[0:10, 0:10] = rlow_ref[:, 0]
    msend[16:26, 0:10] = rup_ref[:, 0]
    msend[32:42, 0:10] = rpiv_ref[:, 0]
    for q in range(4):
        msend[48 + q : 49 + q, :] = weight[:, 128 * q : 128 * (q + 1)]
    for i in range(1, WALL):
        wall_copy(0, i, lambda p: msend, mrecv).start()
    mrecv[w] = msend[...]

    invs[...] = jnp.zeros_like(invs)
    invs[:, 0:EXT] = inv_ref[0]
    row = lax.broadcasted_iota(jnp.int32, (16, 384), 0)
    col = lax.broadcasted_iota(jnp.int32, (16, 384), 1)
    ends = jnp.zeros((16, 384), jnp.float32)
    for v in range(V):
        for q in range(V):
            first = (row == q) & (col == v * CY)
            last = (row == V + q) & (col == v * CY + CY - 1)
            ends = jnp.where(first, lower_ref[v, :, q : q + 1], ends)
            ends = jnp.where(last, upper_ref[v, :, q : q + 1], ends)
    et[...] = ends
    zt = exact(et[...], invs[...], NT)
    zmat[...] = exact(invs[...], et[...], NT)
    for c in range(2):
        kept = (amp_ref[c] * keep).reshape(EXT, 2 * NB)
        found = exact(zt, kept)
        for q in range(4):
            wsend[q, c] = found[:, 128 * q : 128 * (q + 1)]
    for i in range(1, WALL):
        wall_copy(1, i, lambda p: wsend.at[p % 4], wrecv).start()
    wrecv[w] = wsend[w % 4]

    lower_half = lax.broadcasted_iota(jnp.int32, (EXT, 128), 1) < CY
    for v in range(V):
        here = invs[:, 128 * (v // 2) : 128 * (v // 2) + 128]
        there = pltpu.roll(here, CY, 1)
        for r in range(2):
            inside = lower_half if r == 0 else jnp.logical_not(lower_half)
            high, low = split(jnp.where(inside, here if v % 2 == r else there, 0.0))
            ph[r * EXT : (r + 1) * EXT, 128 * v : 128 * (v + 1)] = high
            pl_[r * EXT : (r + 1) * EXT, 128 * v : 128 * (v + 1)] = low
    inv_h, inv_l = split(inv_ref[0])
    for c in range(2):
        source = split(up_ref[c].reshape(EXT, 2 * NB))
        su[:, c * 2 * NB : (c + 1) * 2 * NB] = product((inv_h, inv_l), source, NN)

    for i in range(1, WALL):
        wall_copy(0, i, lambda p: msend, mrecv, True).wait()
    row = lax.broadcasted_iota(jnp.int32, (16, 128), 0)
    col = lax.broadcasted_iota(jnp.int32, (16, 128), 1)
    ahead = []
    for i in range(WALL):
        unit = jnp.where((col == 16 * i + row) & (row < 2 * V), 1.0, 0.0)
        ahead.append(unit if i == 0 else unit - exact(mrecv[i, 0:16, 0:16], ahead[-1]))
    interface = [None] * WALL
    for i in range(WALL - 1, -1, -1):
        value = ahead[i]
        if i < WALL - 1:
            value = value - exact(mrecv[i, 16:32, 0:16], interface[i + 1])
        interface[i] = exact(mrecv[i, 32:48, 0:16], value)
    for i in range(WALL):
        need = jnp.zeros((16, 128), jnp.float32)
        if i > 0:
            need = jnp.where(row < V, pltpu.roll(interface[i - 1], 16 - V, 0), need)
        if i < WALL - 1:
            need = jnp.where((row >= V) & (row < 2 * V), pltpu.roll(interface[i + 1], V, 0), need)
        mm[16 * i : 16 * (i + 1), :] = need
    total_weight = mrecv[0, 48:56, :]
    for i in range(1, WALL):
        total_weight = total_weight + mrecv[i, 48:56, :]
    weight_ref[...] = total_weight + epsilon
    invb_h[...] = jnp.zeros_like(invb_h)
    invb_l[...] = jnp.zeros_like(invb_l)
    for r in range(2):
        for e in range(2):
            for v in range(V):
                to, at = 16 * r + e * V + v, r * EXT + v * CY + e * (CY - 1)
                invb_h[to : to + 1, :] = ph[at : at + 1, :]
                invb_l[to : to + 1, :] = pl_[at : at + 1, :]
    esource[...] = jnp.zeros_like(esource)
    for r in range(2):
        used = keep[:, r * NB : (r + 1) * NB]
        for c in range(2):
            ekeep[16 * r : 16 * (r + 1), c * NB : (c + 1) * NB] = jnp.broadcast_to(used, (16, NB))
            at = c * 2 * NB + r * NB
            for e in range(2):
                for v in range(V):
                    to, o = 16 * r + e * V + v, v * CY + e * (CY - 1)
                    esource[to : to + 1, c * NB : (c + 1) * NB] = su[o : o + 1, at : at + NB] * used
    for i in range(1, WALL):
        wall_copy(1, i, lambda p: wsend.at[p % 4], wrecv, True).wait()

    half = lax.broadcasted_iota(jnp.int32, (GROUP, 128), 1) < CY
    sign = jnp.where(half, 1.0, -1.0)
    wide = lax.broadcasted_iota(jnp.int32, (128, LANES), 1) % 128 < CY
    halves = lax.broadcasted_iota(jnp.int32, (GROUP, LANES), 1) % 128 < CY
    pairs = [(a, b) for a in range(V) for b in range(a + 1, V)]
    weights = [[
        jnp.broadcast_to(
            quad_ref[o, a : a + 1, b : b + 1] + quad_ref[o, b : b + 1, a : a + 1], (8, 128)
        ) for a, b in pairs
    ] for o in range(V)]
    def point(half, z):
        start = PITCH * GROUP * half + z
        picked = jnp.concatenate([
            jnp.concatenate([
                recv1[pl.ds(start + 4 * v + 2 * d, GROUP, stride=PITCH), :] for v in range(V)
            ], axis=1) for d in range(2)
        ], axis=0)
        stacked = jnp.concatenate(
            [jnp.where(wide, picked, 0.0), jnp.where(wide, 0.0, picked)], axis=0
        )
        mixed = product((ch_ref[...], cl_ref[...]), split(stacked), NN)
        field = []
        for v in range(V):
            x = mixed[:, 128 * v : 128 * (v + 1)]
            field.append((pltpu.roll(x, CY, 1) + sign * x).reshape(8, 8, 128))
        force = [jnp.zeros((8, 8, 128), jnp.float32) for _ in range(V)]
        for n, (a, b) in enumerate(pairs):
            both = field[a] * field[b]
            for o in range(V):
                force[o] = force[o] + weights[o][n][None] * both
        force = [x.reshape(GROUP, 128) for x in force]
        folded = jnp.concatenate([pltpu.roll(x, CY, 1) + sign * x for x in force], axis=1)
        stacked = jnp.concatenate(
            [jnp.where(halves, folded, 0.0), jnp.where(halves, 0.0, folded)], axis=0
        )
        found = product((dh_ref[...], dl_ref[...]), split(stacked), NN)
        for v in range(V):
            for d in range(2):
                send2[pl.ds(start + 4 * v + 2 * d, GROUP, stride=PITCH), :] = found[
                    GROUP * d : GROUP * (d + 1), 128 * v : 128 * (v + 1)
                ]

    for half in range(2):
        arrive(half, out)
        for z in range(2):
            point(half, z)
        exchange(half, back)
        recv2[paired(half, me)] = send2[flat(half, me), :]

    sent(out)
    upper_rows = lax.broadcasted_iota(jnp.int32, (32, 8, 128), 1) >= 4
    for half in range(2):
        arrive(half, back)
        even, odd = recv2[32 * half : 32 * half + 32, 0], recv2[32 * half : 32 * half + 32, 1]
        tiles = []
        for v in range(V):
            near, far = (x[:, 8 * (v // 2) : 8 * (v // 2) + 8] for x in (even, odd))
            if v % 2 == 0:
                tiles.append(jnp.where(upper_rows, turn_rows(far), near))
            else:
                tiles.append(jnp.where(upper_rows, far, turn_rows(near)))
        arrived = split(jnp.concatenate([x.reshape(256, 128) for x in tiles], axis=1))
        rows = pl.ds(256 * half, 256)
        table = (th_ref[rows, :], tl_ref[rows, :])
        found = product((invb_h[...], invb_l[...]), arrived, NT)
        found = product(split(found), table, NN)
        if half == 0:
            eacc[...] = found
            found = product((ph[...], pl_[...]), arrived, NT)
            pacc[...] = product(split(found), table, NN)
    edges = (eacc[...] + found) * ekeep[...] + esource[...]
    for r in range(2):
        for c in range(2):
            for q in range(2):
                at = c * NB + q * 128
                bsend[c * 4 + r * 2 + q] = edges[16 * r : 16 * (r + 1), at : at + 128]
    for i in range(1, WALL):
        wall_copy(2, i, lambda p: bsend.at[p], brecv).start()
    brecv[w] = bsend[w]

    pacc[...] += product(split(product((ph[...], pl_[...]), arrived, NT)), table, NN)
    for r in range(2):
        for c in range(2):
            at = c * 2 * NB + r * NB
            acc[:, at : at + NB] = (
                pacc[r * EXT : (r + 1) * EXT, c * NB : (c + 1) * NB] + su[:, at : at + NB]
            ) * keep[:, r * NB : (r + 1) * NB]
    real = jnp.zeros((1, 2 * NB), jnp.float32)
    imag = jnp.zeros((1, 2 * NB), jnp.float32)
    for v in range(V):
        rows = slice(v * CY, (v + 1) * CY)
        k0, k1 = amp_ref[0, v] * keep, amp_ref[1, v] * keep
        c0, c1 = acc[rows, 0 : 2 * NB] - k0, acc[rows, 2 * NB : 4 * NB] - k1
        real = real + jnp.sum(k0 * c0 + k1 * c1, axis=0, keepdims=True)
        imag = imag + jnp.sum(k0 * c1 - k1 * c0, axis=0, keepdims=True)
    for q in range(4):
        lsend[q : q + 1, :] = real[:, 128 * q : 128 * (q + 1)]
        lsend[4 + q : 5 + q, :] = imag[:, 128 * q : 128 * (q + 1)]
    for i in range(1, WALL):
        wall_copy(3, i, lambda p: lsend, lrecv).start()
    lrecv[w] = lsend[...]

    for i in range(1, WALL):
        wall_copy(2, i, lambda p: bsend.at[p], brecv, True).wait()
    need = exact(mm[...], brecv[...].reshape(16 * WALL, 128))
    part = w // 4
    same = wrecv[:, part].reshape(16 * WALL, 128)
    other = wrecv[:, 1 - part].reshape(16 * WALL, 128)
    turn = (2 * part - 1).astype(jnp.float32)
    real = jnp.sum(same * need, axis=0, keepdims=True)
    imag = jnp.sum(other * need, axis=0, keepdims=True) * turn
    nsend[...] = need.reshape(WALL, 16, 128)
    for i in range(WALL):
        nsend[i, 10:11, :] = real
        nsend[i, 11:12, :] = imag
    for i in range(1, WALL):
        wall_copy(4, i, lambda p: nsend.at[p], nrecv).start()
    nrecv[w] = nsend[w]
    for i in range(1, WALL):
        wall_copy(3, i, lambda p: lsend, lrecv, True).wait()
    inner = lrecv[0]
    for i in range(1, WALL):
        inner = inner + lrecv[i]
    inner_ref[...] = inner
    sent(back)
    for i in range(1, WALL):
        wall_copy(4, i, lambda p: nsend.at[p], nrecv, True).wait()


def update(acc_ref, zmat_ref, near_ref, inner_ref, weight_ref, new_hbm, shift_ref, new, sems):
    near = split(jnp.concatenate([near_ref[q] for q in range(WALL)], axis=1))
    stores = []
    for v in range(V):
        rows = slice(v * CY, (v + 1) * CY)
        value = acc_ref[rows, :] - product(split(zmat_ref[rows, :]), near, NN)
        new[0, v] = value[:, 0 : 2 * NB]
        new[1, v] = value[:, 2 * NB : 4 * NB]
        stores.append(pltpu.make_async_copy(new.at[:, v], new_hbm.at[:, v], sems.at[v]))
        stores[-1].start()
    for q in range(4):
        real = inner_ref[q : q + 1, :] - near_ref[q, 10:11, :] - near_ref[4 + q, 10:11, :]
        imag = inner_ref[4 + q : 5 + q, :] - near_ref[q, 11:12, :] - near_ref[4 + q, 11:12, :]
        size = weight_ref[q : q + 1, :]
        shift_ref[0:1, 128 * q : 128 * (q + 1)] = imag / size
        shift_ref[1:2, 128 * q : 128 * (q + 1)] = -real / size
    for store in stores:
        store.wait()


def solution(mesh):
    consts = tables()

    def local(
        amplitudes, upstream, harmonic_mask, quadratic_coefficients, slab_inverse,
        lower_coupling, upper_coupling, reduced_lower, reduced_upper, reduced_pivot,
    ):
        vmem = pl.BlockSpec(memory_space=pltpu.VMEM)
        f32, bf16 = jnp.float32, jnp.bfloat16
        modes = amplitudes.shape[3]
        hbm = pl.BlockSpec(memory_space=pltpu.HBM)

        def turned(block):
            return jnp.transpose(block, (1, 0, 2))

        acc, zmat, near, inner, weight = pl.pallas_call(
            kernel,
            out_shape=(
                jax.ShapeDtypeStruct((EXT, 4 * NB), f32),
                jax.ShapeDtypeStruct((EXT, 16), f32),
                jax.ShapeDtypeStruct((WALL, 16, 128), f32),
                jax.ShapeDtypeStruct((8, 128), f32),
                jax.ShapeDtypeStruct((8, 128), f32),
            ),
            in_specs=[hbm] * 16,
            out_specs=(vmem,) * 5,
            scratch_shapes=[
                pltpu.VMEM((2, V, CY, 2 * NB), f32),
                pltpu.VMEM((2, V, CY, 2 * NB), f32),
                pltpu.VMEM((1, modes), jnp.int32),
                pltpu.VMEM((V, V, V), f32),
                pltpu.VMEM((1, EXT, EXT), f32),
                pltpu.VMEM((V, 1, V), f32),
                pltpu.VMEM((V, 1, V), f32),
                pltpu.VMEM((2 * V, 1, 2 * V), f32),
                pltpu.VMEM((2 * V, 1, 2 * V), f32),
                pltpu.VMEM((2 * V, 1, 2 * V), f32),
                pltpu.VMEM((2 * NB, 2 * NB), bf16),
                pltpu.VMEM((2 * NB, 2 * NB), bf16),
                pltpu.VMEM((GROUP, 4 * GROUP), bf16),
                pltpu.VMEM((GROUP, 4 * GROUP), bf16),
                pltpu.VMEM((2 * GROUP, 2 * GROUP), bf16),
                pltpu.VMEM((2 * GROUP, 2 * GROUP), bf16),
                pltpu.VMEM((LANES, 2 * NB), bf16),
                pltpu.VMEM((LANES, 2 * NB), bf16),
                pltpu.VMEM((GROUP, 2, PITCH, 128), f32),
                pltpu.VMEM((2 * GROUP * PITCH, 128), f32),
                pltpu.VMEM((2 * GROUP * PITCH, 128), f32),
                pltpu.VMEM((GROUP, 2, PITCH, 128), f32),
                pltpu.VMEM((EXT, 384), f32),
                pltpu.VMEM((2 * EXT, LANES), bf16),
                pltpu.VMEM((2 * EXT, LANES), bf16),
                pltpu.VMEM((EXT, 4 * NB), f32),
                pltpu.VMEM((16, 384), f32),
                pltpu.VMEM((32, 2 * NB), f32),
                pltpu.VMEM((32, 2 * NB), f32),
                pltpu.VMEM((32, 2 * NB), f32),
                pltpu.VMEM((2 * EXT, 2 * NB), f32),
                pltpu.VMEM((128, 128), f32),
                pltpu.VMEM((4, 2, 16, 128), f32),
                pltpu.VMEM((WALL, 2, 16, 128), f32),
                pltpu.VMEM((56, 128), f32),
                pltpu.VMEM((WALL, 56, 128), f32),
                pltpu.VMEM((WALL, 16, 128), f32),
                pltpu.VMEM((WALL, 16, 128), f32),
                pltpu.VMEM((8, 128), f32),
                pltpu.VMEM((WALL, 8, 128), f32),
                pltpu.VMEM((WALL, 16, 128), f32),
                pltpu.VMEM((32, LANES), bf16),
                pltpu.VMEM((32, LANES), bf16),
                pltpu.SemaphoreType.DMA((2, GROUP)),
                pltpu.SemaphoreType.DMA((2, GROUP)),
                pltpu.SemaphoreType.DMA((2, GROUP)),
                pltpu.SemaphoreType.DMA((2, GROUP)),
                pltpu.SemaphoreType.DMA((5, WALL)),
                pltpu.SemaphoreType.DMA((5, WALL)),
                pltpu.SemaphoreType.DMA((V + 15,)),
            ],
            compiler_params=pltpu.CompilerParams(
                collective_id=0, has_side_effects=True, vmem_limit_bytes=40 << 20
            ),
        )(*[pltpu.with_memory_space_constraint(x, pltpu.HBM) for x in [
            amplitudes, upstream, harmonic_mask.reshape(1, modes), quadratic_coefficients,
            slab_inverse, turned(lower_coupling), turned(upper_coupling), turned(reduced_lower),
            turned(reduced_upper), turned(reduced_pivot),
            *[jnp.asarray(table) for table in consts],
        ]])
        return pl.pallas_call(
            update,
            out_shape=(
                jax.ShapeDtypeStruct(amplitudes.shape, f32),
                jax.ShapeDtypeStruct((2, modes), f32),
            ),
            in_specs=[vmem] * 5,
            out_specs=(hbm, vmem),
            scratch_shapes=[
                pltpu.VMEM((2, V, CY, 2 * NB), f32),
                pltpu.SemaphoreType.DMA((V,)),
            ],
            compiler_params=pltpu.CompilerParams(vmem_limit_bytes=16 << 20),
        )(acc, zmat, near, inner, weight)

    placed = (
        P(None, None, "wall", ("freq", "span")),
        P(None, None, "wall", ("freq", "span")),
        P(("freq", "span")),
        P(),
        P("wall", None, None),
        P("wall", None, None),
        P("wall", None, None),
        P("wall", None, None),
        P("wall", None, None),
        P("wall", None, None),
    )
    return jax.shard_map(
        local,
        mesh=mesh,
        in_specs=placed,
        out_specs=(P(None, None, "wall", ("freq", "span")), P(None, ("freq", "span"))),
        check_vma=False,
    )
```

```python
import functools
import math

import jax
import jax.numpy as jnp
import numpy as np
from jax import lax
from jax.experimental import pallas as pl
from jax.experimental.pallas import tpu as pltpu
from jax.sharding import PartitionSpec as P

MESH = pl.DeviceIdType.MESH
V = 5
CY = 64
NF = 128
NB = 256
GROUP = 64
WALL = 8
LANES = 2 * V * CY
MESSAGE = 4 * V
PITCH = 24
EXT = V * CY
epsilon = 1e-06
HIGHEST = lax.Precision.HIGHEST
NT = (((1,), (1,)), ((), ()))
NN = (((1,), (0,)), ((), ()))


def split(x):
    high = x.astype(jnp.bfloat16)
    low = (x - high.astype(jnp.float32)).astype(jnp.bfloat16)
    return high, low


def product(a, b, dims):
    (ah, al), (bh, bl) = a, b
    dot = functools.partial(
        lax.dot_general, dimension_numbers=dims, preferred_element_type=jnp.float32
    )
    return dot(ah, bh) + (dot(ah, bl) + dot(al, bh))


def exact(a, b, dims=NN):
    return lax.dot_general(
        a, b, dimension_numbers=dims, precision=HIGHEST, preferred_element_type=jnp.float32
    )


def tables():
    scale = 1.0 / math.sqrt(NF * NB)
    n = np.arange(2 * NB)
    z = 4 * (n // 4 % GROUP) + 2 * (n // (4 * GROUP)) + n % 2
    d = (n // 2) % 2
    phase = 2.0 * np.pi * ((z[:, None] * np.arange(NB)[None, :]) % NB) / NB
    cos, sin = np.cos(phase), np.sin(phase)
    odd = (d == 1)[:, None]
    span = np.concatenate([np.where(odd, sin, cos), np.where(odd, cos, -sin)], axis=1)
    t, place = np.arange(GROUP), np.arange(GROUP)
    j = (place // 8 % 4) * 16 + (place % 8) * 2 + place // 32
    inverse, forward = [], []
    for r in range(2):
        phase = 2.0 * np.pi * ((t[:, None] * (2 * j + r)[None, :]) % NF) / NF
        pair = np.stack([np.cos(phase), -np.sin(phase)], axis=1) * scale
        inverse.append(pair.reshape(GROUP, 2 * GROUP))
        forward.append(pair.reshape(GROUP, 2 * GROUP).T)
    out = []
    for table in (span, np.concatenate(inverse, axis=1), np.concatenate(forward, axis=1)):
        table = table.astype(np.float32)
        high = table.astype(jnp.bfloat16)
        low = (table - high.astype(np.float32)).astype(jnp.bfloat16)
        out += [high, low]
    return out


def kernel(
    amp_hbm, up_hbm, mask_hbm, quad_hbm, inv_hbm, lower_hbm, upper_hbm, rlow_hbm, rup_hbm, rpiv_hbm,
    th_hbm, tl_hbm, ch_hbm, cl_hbm, dh_hbm, dl_hbm,
    acc, zmat, nrecv, inner_ref, weight_ref,
    amp_ref, up_ref, mask_ref, quad_ref, inv_ref, lower_ref, upper_ref, rlow_ref, rup_ref, rpiv_ref,
    th_ref, tl_ref, ch_ref, cl_ref, dh_ref, dl_ref,
    kh, kl, send1, recv1, send2, recv2, invs, ph, pl_, su, et, eacc, esource, ekeep, pacc, mm,
    wsend, wrecv, msend, mrecv, bsend, brecv, lsend, lrecv, nsend, invb_h, invb_l,
    s1, r1, s2, r2, sw, rw, loads,
):
    f, s, w = lax.axis_index("freq"), lax.axis_index("span"), lax.axis_index("wall")
    chip, core = s // 2, s % 2
    me = core * 32 + f * 8 + chip
    barrier = pltpu.get_barrier_semaphore()

    fetch = [
        pltpu.make_async_copy(amp_hbm.at[:, v], amp_ref.at[:, v], loads.at[v]) for v in range(V)
    ]
    for src, dst in (
        (th_hbm, th_ref), (tl_hbm, tl_ref), (mask_hbm, mask_ref), (rlow_hbm, rlow_ref),
        (rup_hbm, rup_ref), (rpiv_hbm, rpiv_ref), (lower_hbm, lower_ref), (upper_hbm, upper_ref),
        (inv_hbm, inv_ref), (up_hbm, up_ref), (quad_hbm, quad_ref), (ch_hbm, ch_ref),
        (cl_hbm, cl_ref), (dh_hbm, dh_ref), (dl_hbm, dl_ref),
    ):
        fetch.append(pltpu.make_async_copy(src, dst, loads.at[len(fetch)]))
    fetch[V + 2].start()
    for copy in fetch[: V + 2] + fetch[V + 3 :]:
        copy.start()

    spot = f * 8 + chip

    def everyone(act, groups=(0, 1)):
        for other in groups:
            c = core if other == 0 else 1 - core

            def one(i, carry):
                p = lax.rem(spot + i, 32)
                act({"freq": lax.div(p, 8), "span": 2 * lax.rem(p, 8) + c}, 32 * c + p)
                return carry

            lax.fori_loop(1 - other, 32, one, 0)

    everyone(
        lambda device, p: pl.semaphore_signal(barrier, inc=1, device_id=device, device_id_type=MESH)
    )
    for i in range(1, WALL):
        pl.semaphore_signal(barrier, inc=1, device_id={"wall": (w + i) % WALL}, device_id_type=MESH)

    def flat(half, index):
        return pl.ds(pl.multiple_of(PITCH * (GROUP * half + index), 8), MESSAGE)

    def paired(half, index):
        return GROUP // 2 * half + lax.div(index, 2), lax.rem(index, 2), pl.ds(0, MESSAGE)

    def message(half, device, p, at, src, dst, src_at, dst_at, ssem, rsem):
        return pltpu.make_async_remote_copy(
            src_ref=src.at[src_at(half, p)], dst_ref=dst.at[dst_at(half, at)],
            send_sem=ssem.at[half, p], recv_sem=rsem.at[half, at], device_id=device,
            device_id_type=MESH,
        )

    out = (send1, recv1, paired, flat, s1, r1)
    back = (send2, recv2, flat, paired, s2, r2)

    def exchange(half, args, groups=(0, 1)):
        everyone(lambda device, p: message(half, device, p, me, *args).start(), groups)

    def arrive(half, args, groups=(0, 1)):
        everyone(lambda device, p: message(half, device, p, p, *args).wait_recv(), groups)

    def sent(args):
        for half in range(2):
            everyone(lambda device, p: message(half, device, p, p, *args).wait_send())

    def wall_copy(step, i, src, dst, inbound=False):
        p = (w + i) % WALL
        return pltpu.make_async_remote_copy(
            src_ref=src(p), dst_ref=dst.at[p if inbound else w], send_sem=sw.at[step, p],
            recv_sem=rw.at[step, p if inbound else w], device_id={"wall": p}, device_id_type=MESH,
        )

    fetch[V + 2].wait()
    keep = mask_ref[...].astype(jnp.float32)

    weight = jnp.zeros((1, 2 * NB), jnp.float32)
    for v in range(V):
        fetch[v].wait()
        for c in range(2):
            block = amp_ref[c, v] * keep
            weight = weight + jnp.sum(block * block, axis=0, keepdims=True)
            high, low = split(block)
            for r in range(2):
                rows = pl.ds(v * 2 * CY + r * CY, CY)
                cols = pl.ds(c * NB, NB)
                kh[rows, cols] = high[:, r * NB : (r + 1) * NB]
                kl[rows, cols] = low[:, r * NB : (r + 1) * NB]

    fetch[V].wait()
    fetch[V + 1].wait()

    upper_rows = lax.broadcasted_iota(jnp.int32, (16, 8, 128), 1) >= 4

    def turn_rows(x):
        return pltpu.roll(x, 4, 1)

    def join(first, second, parity):
        if parity == 0:
            return jnp.where(upper_rows, turn_rows(second), first)
        return jnp.where(upper_rows, second, turn_rows(first))

    def spectral(q):
        rows = pl.ds(pl.multiple_of(128 * q, 128), 128)
        found = product((th_ref[rows, :], tl_ref[rows, :]), (kh[...], kl[...]), NT)
        tiles = [found[:, 128 * v : 128 * (v + 1)].reshape(16, 8, 128) for v in range(V)]
        at = pl.ds(pl.multiple_of(16 * q, 16), 16)
        for parity in range(2):
            for n in range(2):
                send1[at, parity, 8 * n : 8 * n + 8] = join(
                    tiles[2 * n], tiles[2 * n + 1], parity
                )
            send1[at, parity, 16:24] = turn_rows(tiles[4]) if parity else tiles[4]

    for half in range(2):
        for group, parity in enumerate((core, 1 - core)):
            spectral(2 * half + parity)
            if half == 0 and group == 0:
                pl.semaphore_wait(barrier, GROUP - 1 + WALL - 1)
            exchange(half, out, (group,))
    for half in range(2):
        recv1[flat(half, me), :] = send1[paired(half, me)]

    for copy in fetch[V + 3 :]:
        copy.wait()
    msend[...] = jnp.zeros_like(msend)
    msend[0:10, 0:10] = rlow_ref[:, 0]
    msend[16:26, 0:10] = rup_ref[:, 0]
    msend[32:42, 0:10] = rpiv_ref[:, 0]
    for q in range(4):
        msend[48 + q : 49 + q, :] = weight[:, 128 * q : 128 * (q + 1)]
    for i in range(1, WALL):
        wall_copy(0, i, lambda p: msend, mrecv).start()
    mrecv[w] = msend[...]

    invs[...] = jnp.zeros_like(invs)
    invs[:, 0:EXT] = inv_ref[0]
    row = lax.broadcasted_iota(jnp.int32, (16, 384), 0)
    col = lax.broadcasted_iota(jnp.int32, (16, 384), 1)
    ends = jnp.zeros((16, 384), jnp.float32)
    for v in range(V):
        for q in range(V):
            first = (row == q) & (col == v * CY)
            last = (row == V + q) & (col == v * CY + CY - 1)
            ends = jnp.where(first, lower_ref[v, :, q : q + 1], ends)
            ends = jnp.where(last, upper_ref[v, :, q : q + 1], ends)
    et[...] = ends
    zt = exact(et[...], invs[...], NT)
    zmat[...] = exact(invs[...], et[...], NT)
    for c in range(2):
        kept = (amp_ref[c] * keep).reshape(EXT, 2 * NB)
        found = exact(zt, kept)
        for q in range(4):
            wsend[q, c] = found[:, 128 * q : 128 * (q + 1)]
    for i in range(1, WALL):
        wall_copy(1, i, lambda p: wsend.at[p % 4], wrecv).start()
    wrecv[w] = wsend[w % 4]

    lower_half = lax.broadcasted_iota(jnp.int32, (EXT, 128), 1) < CY
    for v in range(V):
        here = invs[:, 128 * (v // 2) : 128 * (v // 2) + 128]
        there = pltpu.roll(here, CY, 1)
        for r in range(2):
            inside = lower_half if r == 0 else jnp.logical_not(lower_half)
            high, low = split(jnp.where(inside, here if v % 2 == r else there, 0.0))
            ph[r * EXT : (r + 1) * EXT, 128 * v : 128 * (v + 1)] = high
            pl_[r * EXT : (r + 1) * EXT, 128 * v : 128 * (v + 1)] = low
    inv_h, inv_l = split(inv_ref[0])
    for c in range(2):
        source = split(up_ref[c].reshape(EXT, 2 * NB))
        su[:, c * 2 * NB : (c + 1) * 2 * NB] = product((inv_h, inv_l), source, NN)

    for i in range(1, WALL):
        wall_copy(0, i, lambda p: msend, mrecv, True).wait()
    row = lax.broadcasted_iota(jnp.int32, (16, 128), 0)
    col = lax.broadcasted_iota(jnp.int32, (16, 128), 1)
    ahead = []
    for i in range(WALL):
        unit = jnp.where((col == 16 * i + row) & (row < 2 * V), 1.0, 0.0)
        ahead.append(unit if i == 0 else unit - exact(mrecv[i, 0:16, 0:16], ahead[-1]))
    interface = [None] * WALL
    for i in range(WALL - 1, -1, -1):
        value = ahead[i]
        if i < WALL - 1:
            value = value - exact(mrecv[i, 16:32, 0:16], interface[i + 1])
        interface[i] = exact(mrecv[i, 32:48, 0:16], value)
    for i in range(WALL):
        need = jnp.zeros((16, 128), jnp.float32)
        if i > 0:
            need = jnp.where(row < V, pltpu.roll(interface[i - 1], 16 - V, 0), need)
        if i < WALL - 1:
            need = jnp.where((row >= V) & (row < 2 * V), pltpu.roll(interface[i + 1], V, 0), need)
        mm[16 * i : 16 * (i + 1), :] = need
    total_weight = mrecv[0, 48:56, :]
    for i in range(1, WALL):
        total_weight = total_weight + mrecv[i, 48:56, :]
    weight_ref[...] = total_weight + epsilon
    invb_h[...] = jnp.zeros_like(invb_h)
    invb_l[...] = jnp.zeros_like(invb_l)
    for r in range(2):
        for e in range(2):
            for v in range(V):
                to, at = 16 * r + e * V + v, r * EXT + v * CY + e * (CY - 1)
                invb_h[to : to + 1, :] = ph[at : at + 1, :]
                invb_l[to : to + 1, :] = pl_[at : at + 1, :]
    esource[...] = jnp.zeros_like(esource)
    for r in range(2):
        used = keep[:, r * NB : (r + 1) * NB]
        for c in range(2):
            ekeep[16 * r : 16 * (r + 1), c * NB : (c + 1) * NB] = jnp.broadcast_to(used, (16, NB))
            at = c * 2 * NB + r * NB
            for e in range(2):
                for v in range(V):
                    to, o = 16 * r + e * V + v, v * CY + e * (CY - 1)
                    esource[to : to + 1, c * NB : (c + 1) * NB] = su[o : o + 1, at : at + NB] * used
    for i in range(1, WALL):
        wall_copy(1, i, lambda p: wsend.at[p % 4], wrecv, True).wait()

    half = lax.broadcasted_iota(jnp.int32, (GROUP, 128), 1) < CY
    sign = jnp.where(half, 1.0, -1.0)
    wide = lax.broadcasted_iota(jnp.int32, (128, LANES), 1) % 128 < CY
    halves = lax.broadcasted_iota(jnp.int32, (GROUP, LANES), 1) % 128 < CY
    pairs = [(a, b) for a in range(V) for b in range(a + 1, V)]
    weights = [[
        jnp.broadcast_to(
            quad_ref[o, a : a + 1, b : b + 1] + quad_ref[o, b : b + 1, a : a + 1], (8, 128)
        ) for a, b in pairs
    ] for o in range(V)]
    def point(half, z):
        start = PITCH * GROUP * half + z
        picked = jnp.concatenate([
            jnp.concatenate([
                recv1[pl.ds(start + 4 * v + 2 * d, GROUP, stride=PITCH), :] for v in range(V)
            ], axis=1) for d in range(2)
        ], axis=0)
        stacked = jnp.concatenate(
            [jnp.where(wide, picked, 0.0), jnp.where(wide, 0.0, picked)], axis=0
        )
        mixed = product((ch_ref[...], cl_ref[...]), split(stacked), NN)
        field = []
        for v in range(V):
            x = mixed[:, 128 * v : 128 * (v + 1)]
            field.append((pltpu.roll(x, CY, 1) + sign * x).reshape(8, 8, 128))
        force = [jnp.zeros((8, 8, 128), jnp.float32) for _ in range(V)]
        for n, (a, b) in enumerate(pairs):
            both = field[a] * field[b]
            for o in range(V):
                force[o] = force[o] + weights[o][n][None] * both
        force = [x.reshape(GROUP, 128) for x in force]
        folded = jnp.concatenate([pltpu.roll(x, CY, 1) + sign * x for x in force], axis=1)
        stacked = jnp.concatenate(
            [jnp.where(halves, folded, 0.0), jnp.where(halves, 0.0, folded)], axis=0
        )
        found = product((dh_ref[...], dl_ref[...]), split(stacked), NN)
        for v in range(V):
            for d in range(2):
                send2[pl.ds(start + 4 * v + 2 * d, GROUP, stride=PITCH), :] = found[
                    GROUP * d : GROUP * (d + 1), 128 * v : 128 * (v + 1)
                ]

    for half in range(2):
        arrive(half, out)
        for z in range(2):
            point(half, z)
        exchange(half, back)
        recv2[paired(half, me)] = send2[flat(half, me), :]

    sent(out)
    for stage in range(4):
        half, group = stage // 2, stage % 2
        parity = core if group == 0 else 1 - core
        arrive(half, back, (group,))
        rows = pl.ds(pl.multiple_of(32 * half + 16 * parity, 16), 16)
        even, odd = recv2[rows, 0], recv2[rows, 1]
        tiles = []
        for v in range(V):
            near, far = (x[:, 8 * (v // 2) : 8 * (v // 2) + 8] for x in (even, odd))
            if v % 2 == 0:
                tiles.append(jnp.where(upper_rows, turn_rows(far), near))
            else:
                tiles.append(jnp.where(upper_rows, far, turn_rows(near)))
        arrived = split(jnp.concatenate([x.reshape(128, 128) for x in tiles], axis=1))
        rows = pl.ds(pl.multiple_of(256 * half + 128 * parity, 128), 128)
        table = (th_ref[rows, :], tl_ref[rows, :])
        found = product((invb_h[...], invb_l[...]), arrived, NT)
        found = product(split(found), table, NN)
        if stage < 3:
            eacc[...] = found if stage == 0 else eacc[...] + found
            found = product((ph[...], pl_[...]), arrived, NT)
            found = product(split(found), table, NN)
            pacc[...] = found if stage == 0 else pacc[...] + found
    edges = (eacc[...] + found) * ekeep[...] + esource[...]
    for r in range(2):
        for c in range(2):
            for q in range(2):
                at = c * NB + q * 128
                bsend[c * 4 + r * 2 + q] = edges[16 * r : 16 * (r + 1), at : at + 128]
    for i in range(1, WALL):
        wall_copy(2, i, lambda p: bsend.at[p], brecv).start()
    brecv[w] = bsend[w]

    pacc[...] += product(split(product((ph[...], pl_[...]), arrived, NT)), table, NN)
    for r in range(2):
        for c in range(2):
            at = c * 2 * NB + r * NB
            acc[:, at : at + NB] = (
                pacc[r * EXT : (r + 1) * EXT, c * NB : (c + 1) * NB] + su[:, at : at + NB]
            ) * keep[:, r * NB : (r + 1) * NB]
    real = jnp.zeros((1, 2 * NB), jnp.float32)
    imag = jnp.zeros((1, 2 * NB), jnp.float32)
    for v in range(V):
        rows = slice(v * CY, (v + 1) * CY)
        k0, k1 = amp_ref[0, v] * keep, amp_ref[1, v] * keep
        c0, c1 = acc[rows, 0 : 2 * NB] - k0, acc[rows, 2 * NB : 4 * NB] - k1
        real = real + jnp.sum(k0 * c0 + k1 * c1, axis=0, keepdims=True)
        imag = imag + jnp.sum(k0 * c1 - k1 * c0, axis=0, keepdims=True)
    for q in range(4):
        lsend[q : q + 1, :] = real[:, 128 * q : 128 * (q + 1)]
        lsend[4 + q : 5 + q, :] = imag[:, 128 * q : 128 * (q + 1)]
    for i in range(1, WALL):
        wall_copy(3, i, lambda p: lsend, lrecv).start()
    lrecv[w] = lsend[...]

    for i in range(1, WALL):
        wall_copy(2, i, lambda p: bsend.at[p], brecv, True).wait()
    need = exact(mm[...], brecv[...].reshape(16 * WALL, 128))
    part = w // 4
    same = wrecv[:, part].reshape(16 * WALL, 128)
    other = wrecv[:, 1 - part].reshape(16 * WALL, 128)
    turn = (2 * part - 1).astype(jnp.float32)
    real = jnp.sum(same * need, axis=0, keepdims=True)
    imag = jnp.sum(other * need, axis=0, keepdims=True) * turn
    nsend[...] = need.reshape(WALL, 16, 128)
    for i in range(WALL):
        nsend[i, 10:11, :] = real
        nsend[i, 11:12, :] = imag
    for i in range(1, WALL):
        wall_copy(4, i, lambda p: nsend.at[p], nrecv).start()
    nrecv[w] = nsend[w]
    for i in range(1, WALL):
        wall_copy(3, i, lambda p: lsend, lrecv, True).wait()
    inner = lrecv[0]
    for i in range(1, WALL):
        inner = inner + lrecv[i]
    inner_ref[...] = inner
    sent(back)
    for i in range(1, WALL):
        wall_copy(4, i, lambda p: nsend.at[p], nrecv, True).wait()


def update(acc_ref, zmat_ref, near_ref, inner_ref, weight_ref, new_hbm, shift_ref, new, sems):
    near = split(jnp.concatenate([near_ref[q] for q in range(WALL)], axis=1))
    stores = []
    for v in range(V):
        rows = slice(v * CY, (v + 1) * CY)
        value = acc_ref[rows, :] - product(split(zmat_ref[rows, :]), near, NN)
        new[0, v] = value[:, 0 : 2 * NB]
        new[1, v] = value[:, 2 * NB : 4 * NB]
        stores.append(pltpu.make_async_copy(new.at[:, v], new_hbm.at[:, v], sems.at[v]))
        stores[-1].start()
    for q in range(4):
        real = inner_ref[q : q + 1, :] - near_ref[q, 10:11, :] - near_ref[4 + q, 10:11, :]
        imag = inner_ref[4 + q : 5 + q, :] - near_ref[q, 11:12, :] - near_ref[4 + q, 11:12, :]
        size = weight_ref[q : q + 1, :]
        shift_ref[0:1, 128 * q : 128 * (q + 1)] = imag / size
        shift_ref[1:2, 128 * q : 128 * (q + 1)] = -real / size
    for store in stores:
        store.wait()


def solution(mesh):
    consts = tables()

    def local(
        amplitudes, upstream, harmonic_mask, quadratic_coefficients, slab_inverse,
        lower_coupling, upper_coupling, reduced_lower, reduced_upper, reduced_pivot,
    ):
        vmem = pl.BlockSpec(memory_space=pltpu.VMEM)
        f32, bf16 = jnp.float32, jnp.bfloat16
        modes = amplitudes.shape[3]
        hbm = pl.BlockSpec(memory_space=pltpu.HBM)

        def turned(block):
            return jnp.transpose(block, (1, 0, 2))

        acc, zmat, near, inner, weight = pl.pallas_call(
            kernel,
            out_shape=(
                jax.ShapeDtypeStruct((EXT, 4 * NB), f32),
                jax.ShapeDtypeStruct((EXT, 16), f32),
                jax.ShapeDtypeStruct((WALL, 16, 128), f32),
                jax.ShapeDtypeStruct((8, 128), f32),
                jax.ShapeDtypeStruct((8, 128), f32),
            ),
            in_specs=[hbm] * 16,
            out_specs=(vmem,) * 5,
            scratch_shapes=[
                pltpu.VMEM((2, V, CY, 2 * NB), f32),
                pltpu.VMEM((2, V, CY, 2 * NB), f32),
                pltpu.VMEM((1, modes), jnp.int32),
                pltpu.VMEM((V, V, V), f32),
                pltpu.VMEM((1, EXT, EXT), f32),
                pltpu.VMEM((V, 1, V), f32),
                pltpu.VMEM((V, 1, V), f32),
                pltpu.VMEM((2 * V, 1, 2 * V), f32),
                pltpu.VMEM((2 * V, 1, 2 * V), f32),
                pltpu.VMEM((2 * V, 1, 2 * V), f32),
                pltpu.VMEM((2 * NB, 2 * NB), bf16),
                pltpu.VMEM((2 * NB, 2 * NB), bf16),
                pltpu.VMEM((GROUP, 4 * GROUP), bf16),
                pltpu.VMEM((GROUP, 4 * GROUP), bf16),
                pltpu.VMEM((2 * GROUP, 2 * GROUP), bf16),
                pltpu.VMEM((2 * GROUP, 2 * GROUP), bf16),
                pltpu.VMEM((LANES, 2 * NB), bf16),
                pltpu.VMEM((LANES, 2 * NB), bf16),
                pltpu.VMEM((GROUP, 2, PITCH, 128), f32),
                pltpu.VMEM(((2 * GROUP + 1) * PITCH, 128), f32),
                pltpu.VMEM(((2 * GROUP + 1) * PITCH, 128), f32),
                pltpu.VMEM((GROUP, 2, PITCH, 128), f32),
                pltpu.VMEM((EXT, 384), f32),
                pltpu.VMEM((2 * EXT, LANES), bf16),
                pltpu.VMEM((2 * EXT, LANES), bf16),
                pltpu.VMEM((EXT, 4 * NB), f32),
                pltpu.VMEM((16, 384), f32),
                pltpu.VMEM((32, 2 * NB), f32),
                pltpu.VMEM((32, 2 * NB), f32),
                pltpu.VMEM((32, 2 * NB), f32),
                pltpu.VMEM((2 * EXT, 2 * NB), f32),
                pltpu.VMEM((128, 128), f32),
                pltpu.VMEM((4, 2, 16, 128), f32),
                pltpu.VMEM((WALL, 2, 16, 128), f32),
                pltpu.VMEM((56, 128), f32),
                pltpu.VMEM((WALL, 56, 128), f32),
                pltpu.VMEM((WALL, 16, 128), f32),
                pltpu.VMEM((WALL, 16, 128), f32),
                pltpu.VMEM((8, 128), f32),
                pltpu.VMEM((WALL, 8, 128), f32),
                pltpu.VMEM((WALL, 16, 128), f32),
                pltpu.VMEM((32, LANES), bf16),
                pltpu.VMEM((32, LANES), bf16),
                pltpu.SemaphoreType.DMA((2, GROUP)),
                pltpu.SemaphoreType.DMA((2, GROUP)),
                pltpu.SemaphoreType.DMA((2, GROUP)),
                pltpu.SemaphoreType.DMA((2, GROUP)),
                pltpu.SemaphoreType.DMA((5, WALL)),
                pltpu.SemaphoreType.DMA((5, WALL)),
                pltpu.SemaphoreType.DMA((V + 15,)),
            ],
            compiler_params=pltpu.CompilerParams(
                collective_id=0, has_side_effects=True, vmem_limit_bytes=40 << 20
            ),
        )(*[pltpu.with_memory_space_constraint(x, pltpu.HBM) for x in [
            amplitudes, upstream, harmonic_mask.reshape(1, modes), quadratic_coefficients,
            slab_inverse, turned(lower_coupling), turned(upper_coupling), turned(reduced_lower),
            turned(reduced_upper), turned(reduced_pivot),
            *[jnp.asarray(table) for table in consts],
        ]])
        return pl.pallas_call(
            update,
            out_shape=(
                jax.ShapeDtypeStruct(amplitudes.shape, f32),
                jax.ShapeDtypeStruct((2, modes), f32),
            ),
            in_specs=[vmem] * 5,
            out_specs=(hbm, vmem),
            scratch_shapes=[
                pltpu.VMEM((2, V, CY, 2 * NB), f32),
                pltpu.SemaphoreType.DMA((V,)),
            ],
            compiler_params=pltpu.CompilerParams(vmem_limit_bytes=16 << 20),
        )(acc, zmat, near, inner, weight)

    placed = (
        P(None, None, "wall", ("freq", "span")),
        P(None, None, "wall", ("freq", "span")),
        P(("freq", "span")),
        P(),
        P("wall", None, None),
        P("wall", None, None),
        P("wall", None, None),
        P("wall", None, None),
        P("wall", None, None),
        P("wall", None, None),
    )
    return jax.shard_map(
        local,
        mesh=mesh,
        in_specs=placed,
        out_specs=(P(None, None, "wall", ("freq", "span")), P(None, ("freq", "span"))),
        check_vma=False,
    )
```
